128 devices in a mesh: sub: 4 (over y), tm: 32 (over z, x, core).
Axes of the slice: x: 4, y: 4, z: 4, core: 2. Of those that a mesh axis runs over, the one named last changes fastest.
Arguments:
- streams: bfloat16 [2, 2160, 131072], P(None, 'sub', 'tm'), may hold values from -6 to 6
- beam_weights: bfloat16 [2, 100, 2160], P(None, None, 'sub'), may hold values from -0.09375 to 0.09375
- code_signs: int32 [32, 16], replicated, may hold values from 0 to 1
- gate_map: int32 [256], replicated, may hold values from 0 to 127, as said below
Outputs:
- profiles: float32 [128, 100, 128], P('tm', 'sub')
The draws below stay inside these ranges and needn't reach their ends.
Inputs may be any that keep to these rules, and one draw needn't show every extreme that they name: `gate_map`: each range gate is named by exactly 2 sections.
All inputs are finite; a program needn't handle non-finite values.
Results may differ from the reference program's by a relative error of at most 0.0041.
Values may be sent and summed in bfloat16 or wider, within the bound.
A program may use at most 128 MiB of HBM per device.

```python
import math
import jax
import jax.numpy as jnp
from jax import lax

CH = 2160
BEAMS = 100
T_DEV = 4096
PKT = 32
IPP_LEN = 512
LAGS = 64
NCODES = 32
NBAUD = 16
BAUD_LEN = 8
SEC_LEN = 2
GATES = 128
NSEC = 256
TIME = 131072
REPS = 4
IPPS = 256
N_TM = 32


def draw_gate_map(key, part):
    order = jax.random.permutation(key, GATES)
    return order[jnp.arange(NSEC) % GATES].astype(jnp.int32)


def place_ends(result, own_key, smallest, high):
    place = [jax.random.randint(jax.random.fold_in(own_key, axis), (), 0, length) for axis, length in enumerate(result.shape)]
    longest = result.shape.index(max(result.shape))
    beside = place[:longest] + [(place[longest] + 1) % result.shape[longest]] + place[longest + 1:]
    return result.at[tuple(place)].set(smallest).at[tuple(beside)].set(high)


def block_levels(key, dims, cuts, smallest, top_value):
    gain = 1.0
    for dim, blocks in cuts:
        steps = jax.random.uniform(jax.random.fold_in(jax.random.fold_in(key, 6), dim), (blocks,), jnp.float32, smallest / len(cuts), top_value / len(cuts))
        gain = gain * jnp.repeat(jnp.exp(steps), dims[dim] // blocks).reshape((-1,) + (1,) * (len(dims) - 1 - dim))
    return gain


def scatter_about(key, extent, deviation, reach, shards=(), held_as=jnp.bfloat16):
    gain = block_levels(key, extent, shards, -0.22, 0.18) if shards else 1.0
    entries = jax.random.normal(key, extent, jnp.float32) * deviation * gain
    return jnp.minimum(jnp.maximum(entries, -reach), reach).astype(held_as)


def setup_inputs(seed: int = 0) -> dict:
    streams_of = jax.random.split(jax.random.key(seed), 5)
    return {
        "streams": scatter_about(streams_of[0], (2, CH, TIME), 1.0, 6.0, ((1, 4), (2, 32))),
        "beam_weights": scatter_about(streams_of[1], (2, BEAMS, CH), (2 * CH) ** -0.5, 0.09375, ((2, 4),)),
        "code_signs": place_ends(jax.random.randint(streams_of[2], (NCODES, NBAUD), 0, 2), jax.random.fold_in(streams_of[2], 1), 0, 1).astype(jnp.int32),
        "gate_map": draw_gate_map(jax.random.fold_in(streams_of[4], 71), 0),
    }


def complex_block(weights):
    w_real = weights[0]
    w_imag = weights[1]
    upper_rows = jnp.concatenate([w_real, -w_imag], 1)
    lower_rows = jnp.concatenate([w_imag, w_real], 1)
    return jnp.stack([upper_rows, lower_rows], 1).reshape(2 * w_real.shape[0], 2 * w_real.shape[1])

def lag_windows(segment):
    offsets = jnp.arange(1, LAGS + 1).astype(jnp.int32)
    return jax.vmap(lambda shift_by: lax.dynamic_slice_in_dim(segment, shift_by, IPP_LEN, 2), out_axes=2)(offsets)

def period_sections(segment, sequence):
    count = segment.shape[0]
    base = segment[:, :, :IPP_LEN]
    later = lag_windows(segment)
    base_real = base[:, 0][:, None, :]
    base_imag = base[:, 1][:, None, :]
    real_part = later[:, 0] * base_real + later[:, 1] * base_imag
    imag_part = later[:, 1] * base_real - later[:, 0] * base_imag
    offsets = jnp.arange(1, LAGS + 1).astype(jnp.int32)
    later_sign = jax.vmap(lambda shift_by: lax.dynamic_slice_in_dim(sequence, shift_by, IPP_LEN, 0))(offsets)
    decode = sequence[:IPP_LEN][None, :] * later_sign
    terms = jnp.stack([real_part, imag_part], 1) * decode[None, None, :, :]
    return terms.reshape(count, 2, LAGS, NSEC, SEC_LEN).sum(-1)

def reference(streams, beam_weights, code_signs, gate_map):
    block = complex_block(beam_weights)
    flat_rows = streams.reshape(2 * CH, TIME)

    def one_block(index):
        columns = lax.dynamic_slice_in_dim(flat_rows, index * T_DEV, T_DEV, 1)
        return jnp.dot(block, columns, preferred_element_type=jnp.float32).astype(jnp.bfloat16)
    arrival = lax.map(one_block, jnp.arange(N_TM).astype(jnp.int32))
    arrival = arrival.reshape(N_TM, BEAMS, 2, T_DEV).transpose(1, 2, 0, 3).reshape(BEAMS, 2, TIME)
    ordered = arrival.reshape(BEAMS, 2, N_TM, N_TM, REPS, PKT).transpose(0, 1, 3, 4, 2, 5).reshape(BEAMS, 2, TIME)
    extended = jnp.concatenate([ordered, jnp.zeros((BEAMS, 2, LAGS), jnp.bfloat16)], 2)
    positions = jnp.arange(IPP_LEN + LAGS)
    baud_hot = ((positions // BAUD_LEN % NBAUD)[:, None] == jnp.arange(NBAUD)[None, :]).astype(jnp.float32)
    sign_table = (2 * code_signs - 1).astype(jnp.float32)
    baud_seq = jnp.dot(sign_table, baud_hot.T, precision=lax.Precision.HIGHEST)

    def add_period(totals, period):
        start = (period * IPP_LEN).astype(jnp.int32)
        segment = lax.dynamic_slice_in_dim(extended, start, IPP_LEN + LAGS, 2).astype(jnp.float32)
        code = (period % NCODES).astype(jnp.int32)
        sequence = lax.dynamic_slice_in_dim(baud_seq, code, 1, 0)[0]
        return (totals + period_sections(segment, sequence), None)
    totals = jnp.zeros((BEAMS, 2, LAGS, NSEC), jnp.float32)
    totals, unused = lax.scan(add_period, totals, jnp.arange(IPPS).astype(jnp.int32))
    gate_hot = (gate_map[:, None] == jnp.arange(GATES)[None, :]).astype(jnp.float32)
    summed = jnp.dot(totals.reshape(BEAMS * 2 * LAGS, NSEC), gate_hot, precision=lax.Precision.HIGHEST)
    scale = 1.0 / math.sqrt(IPPS * IPP_LEN / GATES)
    return summed.reshape(BEAMS, 2 * LAGS, GATES).transpose(2, 0, 1) * scale
```

```python
import math

import jax
import jax.numpy as jnp
from jax import lax
from jax.sharding import PartitionSpec as P

PKT = 32
IPP_LEN = 512
LAGS = 64
NCODES = 32
NBAUD = 16
BAUD_LEN = 8
SEC_LEN = 2
GATES = 128
NSEC = 256


def from_next(block, axis, distance):
    count = lax.axis_size(axis)
    return lax.ppermute(block, axis, [((i + distance) % count, i) for i in range(count)])


def form_beams(streams, beam_weights):
    subs = lax.axis_size("sub")
    w_real = beam_weights[0]
    w_imag = beam_weights[1]
    on_real = jnp.stack([w_real, w_imag], 1).reshape(-1, w_real.shape[1])
    on_imag = jnp.stack([-w_imag, w_real], 1).reshape(-1, w_real.shape[1])
    product = jnp.dot(on_real, streams[0], preferred_element_type=jnp.float32) + jnp.dot(
        on_imag, streams[1], preferred_element_type=jnp.float32
    )
    parts = product.reshape(subs, -1, streams.shape[2])
    arrived = lax.all_to_all(parts, "sub", split_axis=0, concat_axis=0, tiled=True)
    return arrived.sum(axis=0).astype(jnp.bfloat16)


def body(streams, beam_weights, code_signs, gate_map):
    tms = lax.axis_size("tm")
    here = lax.axis_index("tm")
    early = form_beams(streams, beam_weights)
    beams_here = early.shape[0] // 2
    chunks = early.shape[1] // PKT
    held = early.reshape(beams_here, 2, chunks, PKT)
    pieces = [held]
    for distance in (1, 2):
        later = from_next(held, "tm", distance)
        moved = jnp.concatenate([later[:, :, 1:], jnp.zeros_like(later[:, :, :1])], 2)
        pieces.append(jnp.where(here + distance >= tms, moved, later))
    wide = jnp.concatenate(pieces, 3)
    width = wide.shape[3]
    groups = IPP_LEN // PKT
    codes = (jnp.arange(chunks) * (tms * PKT // IPP_LEN) + here // groups) % NCODES
    bauds = (here * (PKT // BAUD_LEN) + jnp.arange(width) // BAUD_LEN) % NBAUD
    signs = (2 * code_signs - 1)[codes][:, bauds].astype(jnp.bfloat16)
    coded = wide * signs
    base = coded[..., :PKT]
    turned = jnp.stack([-base[:, 1], base[:, 0]], 1)
    both = jnp.stack([base, turned], 1)
    gram = jnp.einsum("bqpco,bpcw->bqow", both, coded, preferred_element_type=jnp.float32)
    flat = gram.reshape(beams_here, 2, PKT * width)
    flat = jnp.pad(flat, ((0, 0), (0, 0), (0, PKT)))
    skewed = flat.reshape(beams_here, 2, PKT, width + 1)[..., 1 : LAGS + 1]
    secs = PKT // SEC_LEN
    sections = skewed.reshape(beams_here, 2, secs, SEC_LEN, LAGS).sum(3)
    gates = lax.dynamic_slice_in_dim(gate_map, (here % groups) * secs, secs)
    hot = (jnp.arange(GATES)[:, None] == gates[None, :]).astype(jnp.float32)
    scale = 1.0 / math.sqrt(tms * chunks * PKT / GATES)
    term = jnp.einsum("gs,bqsl->gbql", hot, sections * scale, precision=lax.Precision.HIGHEST)
    parts = term.reshape(tms, GATES // tms, beams_here, 2 * LAGS)
    arrived = lax.all_to_all(parts, "tm", split_axis=0, concat_axis=0, tiled=True)
    return arrived.sum(axis=0)


def solution(mesh):
    placed = (P(None, "sub", "tm"), P(None, None, "sub"), P(), P())
    return jax.shard_map(
        body, mesh=mesh, in_specs=placed, out_specs=P("tm", "sub", None), check_vma=False
    )
```

```python
import functools
import math

import jax
import jax.numpy as jnp
from jax import lax
from jax.experimental import pallas as pl
from jax.experimental.pallas import tpu as pltpu
from jax.sharding import PartitionSpec as P

PKT = 32
IPP_LEN = 512
LAGS = 64
NCODES = 32
NBAUD = 16
BAUD_LEN = 8
SEC_LEN = 2
GATES = 128
NSEC = 256
LANES = 128
SUBS = 4
TMS = 32
BEAMS = 25
T_DEV = 4096
GROUPS = T_DEV // LANES
ROWS = 2 * GROUPS
PAD = 112
CHUNK = 5
STEPS = BEAMS // CHUNK
PART = CHUNK * ROWS
HALF = PART // 2
BLOCK = 256
BLOCKS = T_DEV // BLOCK
WIDE = BEAMS * LANES
MESH = pl.DeviceIdType.MESH


def iota(shape, dim):
    return lax.broadcasted_iota(jnp.int32, shape, dim)


def kernel(
    streams, weights, code_signs, gate_map, out,
    held, block_rows, sums, early, first, second, beams, next1, next2, signs,
    coded, skewed, own_sec, pair_sec, row_sec, picked, gate_part, core_part,
    in_sem, a_send, a_recv, b_send, b_recv, h_send, h_recv,
    p_send, p_recv, z_send, z_recv, x_send, x_recv, c_send, c_recv,
):
    y = lax.axis_index("sub")
    d = lax.axis_index("tm")
    z = d // 8
    x = (d // 2) % 4
    core = d % 2
    half = d // 16

    def ring(step):
        return (y, lax.rem(d + step + TMS, TMS))

    def sub_to(step):
        return (lax.rem(y + step, SUBS), d)

    def z_to(step):
        return (y, lax.rem(z + step, 4) * 8 + x * 2 + core)

    def x_to(step):
        return (y, z * 8 + lax.rem(x + step, 4) * 2 + core)

    other_core = (y, d + 1 - 2 * core)

    def fetch(i):
        cols = pl.ds(pl.multiple_of(i * BLOCK, BLOCK), BLOCK)
        return pltpu.make_async_copy(
            streams.at[:, :, cols], held.at[:, :, cols], in_sem.at[i]
        )

    for i in range(BLOCKS):
        fetch(i).start()

    barrier = pltpu.get_barrier_semaphore()
    met = [sub_to(1), sub_to(3), ring(-1), ring(-2), ring(1), ring(2)]
    met += [z_to(1), z_to(2), z_to(3), x_to(1), x_to(2), x_to(3), other_core]
    for device in met:
        pl.semaphore_signal(barrier, inc=1, device_id=device, device_id_type=MESH)

    w_real = weights[0]
    w_imag = weights[1]
    block_rows[...] = jnp.zeros_like(block_rows)
    block_rows[0, 0 : w_real.shape[0], :] = w_real
    block_rows[0, PAD : PAD + w_real.shape[0], :] = w_imag
    block_rows[1, 0 : w_real.shape[0], :] = -w_imag
    block_rows[1, PAD : PAD + w_real.shape[0], :] = w_real

    def form(i, carry):
        fetch(i).wait()
        cols = pl.ds(pl.multiple_of(i * BLOCK, BLOCK), BLOCK)
        product = jnp.dot(
            block_rows[0], held[0, :, cols], preferred_element_type=jnp.float32
        ) + jnp.dot(block_rows[1], held[1, :, cols], preferred_element_type=jnp.float32)
        for h in range(BLOCK // LANES):
            for part in range(2):
                sums[pl.ds(part * GROUPS + i * (BLOCK // LANES) + h, 104, stride=ROWS), :] = product[
                    part * PAD : part * PAD + 104, h * LANES : (h + 1) * LANES
                ]
        return carry

    lax.fori_loop(0, BLOCKS, form, 0)
    pl.semaphore_wait(barrier, len(met))

    def rows_of(owner, step):
        return pl.multiple_of((owner * BEAMS + step * CHUNK) * ROWS, ROWS)

    def send_far(step, way):
        start = rows_of(lax.rem(y + 2, SUBS), step) + way * HALF
        return pltpu.make_async_remote_copy(
            src_ref=sums.at[pl.ds(start, HALF), :],
            dst_ref=early.at[step, way],
            send_sem=a_send.at[step, way],
            recv_sem=a_recv.at[step, way],
            device_id=sub_to(1 if way == 0 else 3),
            device_id_type=MESH,
        )

    def send_near(step, way):
        owner = lax.rem(y + (1 if way == 0 else 3), SUBS)
        landing = first if way == 0 else second
        return pltpu.make_async_remote_copy(
            src_ref=sums.at[pl.ds(rows_of(owner, step), PART), :],
            dst_ref=landing.at[step],
            send_sem=b_send.at[step, way],
            recv_sem=b_recv.at[step, way],
            device_id=sub_to(1 if way == 0 else 3),
            device_id_type=MESH,
        )

    def send_edge(step, way):
        landing = next1 if way == 0 else next2
        rows = pl.ds(step * PART, PART)
        return pltpu.make_async_remote_copy(
            src_ref=beams.at[rows, :],
            dst_ref=landing.at[rows, :],
            send_sem=h_send.at[step, way],
            recv_sem=h_recv.at[step, way],
            device_id=ring(-1 - way),
            device_id_type=MESH,
        )

    row = iota((256, NCODES), 0)
    code_of = lax.rem(
        2 * lax.rem(4 * lax.rem(row, GROUPS) + row // 64, 16) + half, NCODES
    )
    code_hot = (code_of == iota((256, NCODES), 1)).astype(jnp.bfloat16)
    lane16 = iota((NBAUD, LANES), 1)
    baud_hot = jnp.where(
        (lax.rem(4 * d + lane16 // BAUD_LEN, NBAUD) == iota((NBAUD, LANES), 0)) & (lane16 < 96),
        1.0,
        0.0,
    ).astype(jnp.bfloat16)
    table = (2 * code_signs[...] - 1).astype(jnp.float32).astype(jnp.bfloat16)
    by_code = jnp.dot(code_hot, table, preferred_element_type=jnp.float32).astype(jnp.bfloat16)
    signs[...] = jnp.dot(by_code, baud_hot, preferred_element_type=jnp.float32).astype(jnp.bfloat16)

    def relay(step):
        for way in range(2):
            send_far(step, way).wait_recv()
            owner = lax.rem(y + (1 if way == 0 else 3), SUBS)
            rows = pl.ds(rows_of(owner, step) + way * HALF, HALF)
            sums[rows, :] = sums[rows, :] + early[step, way]
            send_near(step, way).start()

    def settle(step):
        for way in range(2):
            send_near(step, way).wait_recv()
        total = sums[pl.ds(rows_of(y, step), PART), :] + first[step] + second[step]
        beams[pl.ds(step * PART, PART), :] = total.astype(jnp.bfloat16)
        for way in range(2):
            send_edge(step, way).start()

    lane = iota((ROWS, LANES), 1)

    def passed_end(ref, step):
        rows = pl.ds(step * PART, PART)
        turned = pltpu.roll(ref[rows, :].astype(jnp.float32), 96, 1)
        above = pltpu.roll(turned, PART - 1, 0)
        last = lax.rem(iota((PART, LANES), 0), GROUPS) == GROUPS - 1
        new = jnp.where(iota((PART, LANES), 1) < 96, turned, jnp.where(last, 0.0, above))
        ref[rows, :] = new.astype(jnp.bfloat16)

    def correlate(step):
        for way in range(2):
            send_edge(step, way).wait_recv()

        @pl.when(d >= TMS - 1)
        def _():
            passed_end(next1, step)

        @pl.when(d >= TMS - 2)
        def _():
            passed_end(next2, step)

        def one_beam(k, carry):
            beam = step * CHUNK + k
            rows = pl.ds(pl.multiple_of(beam * ROWS, ROWS), ROWS)
            here, n1, n2 = beams[rows, :], next1[rows, :], next2[rows, :]
            for c in range(4):
                mixed = jnp.where(
                    lane < 32,
                    pltpu.roll(here, (128 - 32 * c) % 128, 1) if c else here,
                    jnp.where(
                        lane < 64,
                        pltpu.roll(n1, (160 - 32 * c) % 128, 1) if c != 1 else n1,
                        pltpu.roll(n2, (192 - 32 * c) % 128, 1) if c != 2 else n2,
                    ),
                )
                mixed = mixed * signs[c * ROWS : (c + 1) * ROWS, :]
                for part in range(2):
                    coded[part * 128 + c * GROUPS : part * 128 + (c + 1) * GROUPS, :] = mixed[
                        part * GROUPS : (part + 1) * GROUPS
                    ]
            later = coded[...]
            turned = jnp.concatenate([-later[128:], later[:128]], 0)
            lane_all = iota((256, LANES), 1)
            base = jnp.where(lane_all < 32, later, pltpu.roll(turned, 32, 1))
            gram = lax.dot_general(
                base, later, (((0,), (0,)), ((), ())), preferred_element_type=jnp.float32
            )
            gram = gram[0:64]
            offset = iota((64, LANES), 0)
            for bit in (1, 2, 4, 8, 16):
                gram = jnp.where((offset & bit) > 0, pltpu.roll(gram, LANES - bit, 1), gram)
            real = pltpu.roll(gram[0:32], 127, 1)
            imag = pltpu.roll(gram[32:64], 63, 1)
            skewed[...] = jnp.where(iota((32, LANES), 1) < LAGS, real, imag)
            pairs = skewed[pl.ds(0, 16, stride=2), :] + skewed[pl.ds(1, 16, stride=2), :]
            cols = pl.ds(pl.multiple_of(beam * LANES, LANES), LANES)
            own_sec[0, :, cols] = pairs[:8]
            own_sec[1, :, cols] = pairs[8:]
            return carry

        lax.fori_loop(0, CHUNK, one_beam, 0)

    for way in range(2):
        send_far(0, way).start()
    for s in range(STEPS + 2):
        if s + 1 < STEPS:
            for way in range(2):
                send_far(s + 1, way).start()
        if s < STEPS:
            relay(s)
        if 1 <= s <= STEPS:
            settle(s - 1)
        if 2 <= s:
            correlate(s - 2)

    to_pair = pltpu.make_async_remote_copy(
        src_ref=own_sec.at[1 - half],
        dst_ref=pair_sec,
        send_sem=p_send,
        recv_sem=p_recv,
        device_id=z_to(2),
        device_id_type=MESH,
    )
    to_pair.start()
    to_pair.wait_recv()
    row_sec[z] = own_sec[half] + pair_sec[...]

    def to_z(i):
        return pltpu.make_async_remote_copy(
            src_ref=row_sec.at[z],
            dst_ref=row_sec.at[z],
            send_sem=z_send.at[i - 1],
            recv_sem=z_recv.at[i - 1],
            device_id=z_to(i),
            device_id_type=MESH,
        )

    for i in (1, 2, 3):
        to_z(i).start()
    gate_row = z * 32 + iota((32, NSEC), 0)
    named = (gate_map[...] == gate_row).astype(jnp.bfloat16)
    col = iota((NSEC, 32), 1)
    col_z = col // 8
    section = 16 * (lax.rem(col_z, 2) * 8 + x * 2 + core) + 8 * (col_z // 2) + lax.rem(col, 8)
    chosen = (iota((NSEC, 32), 0) == section).astype(jnp.bfloat16)
    gate_hot = jnp.dot(named, chosen, preferred_element_type=jnp.float32)
    for i in (1, 2, 3):
        to_z(i).wait_recv()
    scale = 1.0 / math.sqrt(TMS * T_DEV / GATES)
    gathered = row_sec[...].reshape(32, WIDE)
    picked[...] = jnp.dot(gate_hot, gathered * scale, precision=lax.Precision.HIGHEST).reshape(
        4, 8, WIDE
    )

    def to_x(i):
        return pltpu.make_async_remote_copy(
            src_ref=picked.at[lax.rem(x + i, 4)],
            dst_ref=gate_part.at[i - 1],
            send_sem=x_send.at[i - 1],
            recv_sem=x_recv.at[i - 1],
            device_id=x_to(i),
            device_id_type=MESH,
        )

    for i in (1, 2, 3):
        to_x(i).start()
    for i in (1, 2, 3):
        to_x(i).wait_recv()
    core_part[0] = picked[x] + gate_part[0] + gate_part[1] + gate_part[2]
    to_core = pltpu.make_async_remote_copy(
        src_ref=core_part.at[0],
        dst_ref=core_part.at[1],
        send_sem=c_send,
        recv_sem=c_recv,
        device_id=other_core,
        device_id_type=MESH,
    )
    to_core.start()
    to_core.wait_recv()
    out[...] = core_part[0] + core_part[1]

    for step in range(STEPS):
        for way in range(2):
            send_far(step, way).wait_send()
            send_near(step, way).wait_send()
            send_edge(step, way).wait_send()
    to_pair.wait_send()
    for i in (1, 2, 3):
        to_z(i).wait_send()
        to_x(i).wait_send()
    to_core.wait_send()


def body(streams, beam_weights, code_signs, gate_map):
    dma = pltpu.SemaphoreType.DMA
    f32, bf16 = jnp.float32, jnp.bfloat16
    vmem = pl.BlockSpec(memory_space=pltpu.VMEM)
    summed = pl.pallas_call(
        kernel,
        out_shape=jax.ShapeDtypeStruct((8, WIDE), f32),
        in_specs=[pl.BlockSpec(memory_space=pl.ANY), vmem, vmem, vmem],
        out_specs=vmem,
        scratch_shapes=[
            pltpu.VMEM(streams.shape, bf16),
            pltpu.VMEM((2, 2 * PAD, streams.shape[1]), bf16),
            pltpu.VMEM((104 * ROWS, LANES), f32),
            pltpu.VMEM((STEPS, 2, HALF, LANES), f32),
            pltpu.VMEM((STEPS, PART, LANES), f32),
            pltpu.VMEM((STEPS, PART, LANES), f32),
            pltpu.VMEM((BEAMS * ROWS, LANES), bf16),
            pltpu.VMEM((BEAMS * ROWS, LANES), bf16),
            pltpu.VMEM((BEAMS * ROWS, LANES), bf16),
            pltpu.VMEM((256, LANES), bf16),
            pltpu.VMEM((256, LANES), bf16),
            pltpu.VMEM((32, LANES), f32),
            pltpu.VMEM((2, 8, WIDE), f32),
            pltpu.VMEM((8, WIDE), f32),
            pltpu.VMEM((4, 8, WIDE), f32),
            pltpu.VMEM((4, 8, WIDE), f32),
            pltpu.VMEM((3, 8, WIDE), f32),
            pltpu.VMEM((2, 8, WIDE), f32),
            dma((BLOCKS,)),
            dma((STEPS, 2)), dma((STEPS, 2)), dma((STEPS, 2)), dma((STEPS, 2)),
            dma((STEPS, 2)), dma((STEPS, 2)),
            dma, dma, dma((3,)), dma((3,)), dma((3,)), dma((3,)), dma, dma,
        ],
        compiler_params=pltpu.CompilerParams(
            collective_id=0, has_side_effects=True, vmem_limit_bytes=48 * 2**20
        ),
    )(streams, beam_weights, code_signs, gate_map.reshape(1, NSEC))
    core = lax.axis_index("tm") % 2
    mine = lax.dynamic_slice_in_dim(summed, 4 * core, 4, 0)
    return mine.reshape(4, BEAMS, LANES)


def solution(mesh):
    placed = (P(None, "sub", "tm"), P(None, None, "sub"), P(), P())
    return jax.shard_map(
        body, mesh=mesh, in_specs=placed, out_specs=P("tm", "sub", None), check_vma=False
    )
```

```python
import functools
import math

import jax
import jax.numpy as jnp
from jax import lax
from jax.experimental import pallas as pl
from jax.experimental.pallas import tpu as pltpu
from jax.sharding import PartitionSpec as P

PKT = 32
IPP_LEN = 512
LAGS = 64
NCODES = 32
NBAUD = 16
BAUD_LEN = 8
SEC_LEN = 2
GATES = 128
NSEC = 256
LANES = 128
SUBS = 4
TMS = 32
BEAMS = 25
T_DEV = 4096
GROUPS = T_DEV // LANES
ROWS = 2 * GROUPS
WEIGHT_TILES = 5
CHUNK = 5
STEPS = BEAMS // CHUNK
PART = CHUNK * ROWS
HALF = PART // 2
BLOCK = 256
WIDE = BEAMS * LANES
BITS = 14.0
MESH = pl.DeviceIdType.MESH


def iota(shape, dim):
    return lax.broadcasted_iota(jnp.int32, shape, dim)


def kernel(
    streams, weights, code_signs, gate_map, out,
    held, plain, block_rows, sums, early, first, second, beams, next1, next2, signs,
    coded, skewed, row_sec, picked, gate_part, far_out, near_out,
    in_sem, a_send, a_recv, b_send, b_recv, h_send, h_recv, z_send, z_recv, g_send, g_recv,
):
    y = lax.axis_index("sub")
    d = lax.axis_index("tm")
    z = d // 8
    half = d // 16

    def ring(step):
        return (y, lax.rem(d + step + TMS, TMS))

    def sub_to(step):
        return (lax.rem(y + step, SUBS), d)

    def z_to(step):
        return (y, lax.rem(z + step, 4) * 8 + lax.rem(d, 8))

    def row_to(step):
        return (y, z * 8 + lax.rem(d + step, 8))

    def fetch(i):
        return pltpu.make_async_copy(streams.at[:, i], held.at[i], in_sem.at[i])

    for i in range(GROUPS):
        fetch(i).start()

    barrier = pltpu.get_barrier_semaphore()
    met = [sub_to(1), sub_to(3), ring(-1), ring(-2), ring(1), ring(2)]
    met += [z_to(i) for i in (1, 2, 3)] + [row_to(i) for i in range(1, 8)]
    for device in met:
        pl.semaphore_signal(barrier, inc=1, device_id=device, device_id_type=MESH)

    channels = weights.shape[2]
    stacked = weights[...].reshape(2 * weights.shape[0], channels)
    wide_rows = stacked.astype(jnp.float32)
    count = wide_rows.shape[0]
    odd = lax.rem(iota(wide_rows.shape, 0), 2) == 1
    turned_rows = jnp.where(odd, pltpu.roll(wide_rows, 1, 0), -pltpu.roll(wide_rows, count - 1, 0))
    plain[...] = jnp.zeros_like(plain)
    plain[0, :, 0:channels] = stacked
    plain[1, :, 0:channels] = turned_rows.astype(jnp.bfloat16)
    source = iota((BLOCK, BLOCK), 0)
    spread = (
        2 * lax.rem(source, LANES) + source // LANES == iota((BLOCK, BLOCK), 1)
    ).astype(jnp.bfloat16)
    for t in range(WEIGHT_TILES):
        cols = slice(t * LANES, (t + 1) * LANES)
        pair = jnp.concatenate([plain[0, :, cols], plain[1, :, cols]], 1)
        block_rows[:, t * BLOCK : (t + 1) * BLOCK] = jnp.dot(
            pair, spread, preferred_element_type=jnp.float32
        ).astype(jnp.bfloat16)
    samples = held.reshape(GROUPS, 2 * channels, LANES)

    def form(i, carry):
        for h in range(2):
            fetch(2 * i + h).wait()
        product = jnp.dot(
            block_rows[:, 0 : 2 * channels],
            jnp.concatenate([samples[2 * i], samples[2 * i + 1]], 1),
            preferred_element_type=jnp.float32,
        )
        for h in range(2):
            sums[pl.ds(2 * i + h, count, stride=GROUPS), :] = product[:, h * LANES : (h + 1) * LANES]
        top = jnp.max(jnp.abs(product).reshape(count // 8, 8, BLOCK), axis=0)
        return jnp.maximum(carry, top)

    top = lax.fori_loop(0, GROUPS // 2, form, jnp.zeros((8, BLOCK), jnp.float32))
    top = jnp.maximum(jnp.max(top, axis=(0, 1), keepdims=True), 1e-30)
    level = jnp.broadcast_to(jnp.ceil(jnp.log2(top)), (16, LANES))
    pl.semaphore_wait(barrier, len(met))

    def rows_of(owner, step):
        return pl.multiple_of((owner * BEAMS + step * CHUNK) * ROWS, ROWS)

    def packed(value, power):
        steps = value.reshape(-1, 16, LANES) * jnp.exp2(BITS - power)[None]
        return jnp.round(steps).astype(jnp.int32).astype(jnp.int16).reshape(-1, LANES)

    def unpacked(ref, count):
        power = ref[count : count + 16, :].astype(jnp.int32).astype(jnp.float32)
        steps = ref[0:count, :].astype(jnp.int32).astype(jnp.float32)
        value = steps.reshape(-1, 16, LANES) * jnp.exp2(power - BITS)[None]
        return value.reshape(count, LANES), power

    def ways(way):
        return 1 if way == 0 else 3

    def send_far(step, way):
        return pltpu.make_async_remote_copy(
            src_ref=far_out.at[step, way],
            dst_ref=early.at[step, way],
            send_sem=a_send.at[step, way],
            recv_sem=a_recv.at[step, way],
            device_id=sub_to(ways(way)),
            device_id_type=MESH,
        )

    def send_near(step, way):
        landing = first if way == 0 else second
        return pltpu.make_async_remote_copy(
            src_ref=near_out.at[step, way],
            dst_ref=landing.at[step],
            send_sem=b_send.at[step, way],
            recv_sem=b_recv.at[step, way],
            device_id=sub_to(ways(way)),
            device_id_type=MESH,
        )

    def launch(step):
        for way in range(2):
            start = rows_of(lax.rem(y + 2, SUBS), step) + way * HALF
            far_out[step, way, 0:HALF, :] = packed(sums[pl.ds(start, HALF), :], level)
            far_out[step, way, HALF : HALF + 16, :] = level.astype(jnp.int32).astype(jnp.int16)
            send_far(step, way).start()

    def send_edge(step, way):
        landing = next1 if way == 0 else next2
        rows = pl.ds(step * PART, PART)
        return pltpu.make_async_remote_copy(
            src_ref=beams.at[rows, :],
            dst_ref=landing.at[rows, :],
            send_sem=h_send.at[step, way],
            recv_sem=h_recv.at[step, way],
            device_id=ring(-1 - way),
            device_id_type=MESH,
        )

    row = iota((256, NCODES), 0)
    code_of = lax.rem(
        2 * lax.rem(4 * lax.rem(row, GROUPS) + row // 64, 16) + half, NCODES
    )
    code_hot = (code_of == iota((256, NCODES), 1)).astype(jnp.bfloat16)
    lane16 = iota((NBAUD, LANES), 1)
    baud_hot = jnp.where(
        (lax.rem(4 * d + lane16 // BAUD_LEN, NBAUD) == iota((NBAUD, LANES), 0)) & (lane16 < 96),
        1.0,
        0.0,
    ).astype(jnp.bfloat16)
    table = (2 * code_signs[...] - 1).astype(jnp.float32).astype(jnp.bfloat16)
    by_code = jnp.dot(code_hot, table, preferred_element_type=jnp.float32).astype(jnp.bfloat16)
    signs[...] = jnp.dot(by_code, baud_hot, preferred_element_type=jnp.float32).astype(jnp.bfloat16)

    def relay(step):
        for way in range(2):
            send_far(step, way).wait_recv()
            start = rows_of(lax.rem(y + ways(way), SUBS), step)
            passed, power = unpacked(early.at[step, way], HALF)
            both = jnp.maximum(power, level) + 1
            mine = slice(way * HALF, (way + 1) * HALF)
            rest = slice((1 - way) * HALF, (2 - way) * HALF)
            near_out[step, way, mine, :] = packed(
                sums[pl.ds(start + way * HALF, HALF), :] + passed, both
            )
            near_out[step, way, rest, :] = packed(
                sums[pl.ds(start + (1 - way) * HALF, HALF), :], both
            )
            near_out[step, way, PART : PART + 16, :] = both.astype(jnp.int32).astype(jnp.int16)
            send_near(step, way).start()

    def settle(step):
        for way in range(2):
            send_near(step, way).wait_recv()
        total = sums[pl.ds(rows_of(y, step), PART), :]
        total += unpacked(first.at[step], PART)[0] + unpacked(second.at[step], PART)[0]
        beams[pl.ds(step * PART, PART), :] = total.astype(jnp.bfloat16)
        for way in range(2):
            send_edge(step, way).start()

    lane = iota((ROWS, LANES), 1)

    def passed_end(ref, step):
        rows = pl.ds(step * PART, PART)
        turned = pltpu.roll(ref[rows, :].astype(jnp.float32), 96, 1)
        above = pltpu.roll(turned, PART - 1, 0)
        last = lax.rem(iota((PART, LANES), 0), GROUPS) == GROUPS - 1
        new = jnp.where(iota((PART, LANES), 1) < 96, turned, jnp.where(last, 0.0, above))
        ref[rows, :] = new.astype(jnp.bfloat16)

    def correlate(step):
        for way in range(2):
            send_edge(step, way).wait_recv()

        @pl.when(d >= TMS - 1)
        def _():
            passed_end(next1, step)

        @pl.when(d >= TMS - 2)
        def _():
            passed_end(next2, step)

        def one_beam(k, carry):
            beam = step * CHUNK + k
            rows = pl.ds(pl.multiple_of(beam * ROWS, ROWS), ROWS)
            here, n1, n2 = beams[rows, :], next1[rows, :], next2[rows, :]
            for c in range(4):
                mixed = jnp.where(
                    lane < 32,
                    pltpu.roll(here, (128 - 32 * c) % 128, 1) if c else here,
                    jnp.where(
                        lane < 64,
                        pltpu.roll(n1, (160 - 32 * c) % 128, 1) if c != 1 else n1,
                        pltpu.roll(n2, (192 - 32 * c) % 128, 1) if c != 2 else n2,
                    ),
                )
                mixed = mixed * signs[c * ROWS : (c + 1) * ROWS, :]
                for part in range(2):
                    coded[part * 128 + c * GROUPS : part * 128 + (c + 1) * GROUPS, :] = mixed[
                        part * GROUPS : (part + 1) * GROUPS
                    ]
            later = coded[...]
            turned = jnp.concatenate([-later[128:], later[:128]], 0)
            lane_all = iota((256, LANES), 1)
            base = jnp.where(lane_all < 32, later, pltpu.roll(turned, 32, 1))
            gram = lax.dot_general(
                base, later, (((0,), (0,)), ((), ())), preferred_element_type=jnp.float32
            )
            gram = gram[0:64]
            offset = iota((64, LANES), 0)
            for bit in (1, 2, 4, 8, 16):
                gram = jnp.where((offset & bit) > 0, pltpu.roll(gram, LANES - bit, 1), gram)
            real = pltpu.roll(gram[0:32], 127, 1)
            imag = pltpu.roll(gram[32:64], 63, 1)
            skewed[...] = jnp.where(iota((32, LANES), 1) < LAGS, real, imag)
            pairs = skewed[pl.ds(0, 16, stride=2), :] + skewed[pl.ds(1, 16, stride=2), :]
            cols = pl.ds(pl.multiple_of(k * LANES, LANES), LANES)
            row_sec[step, z, :, cols] = pairs
            return carry

        lax.fori_loop(0, CHUNK, one_beam, 0)

    def send_z(step, i):
        return pltpu.make_async_remote_copy(
            src_ref=row_sec.at[step, z],
            dst_ref=row_sec.at[step, z],
            send_sem=z_send.at[step, i - 1],
            recv_sem=z_recv.at[step, i - 1],
            device_id=z_to(i),
            device_id_type=MESH,
        )

    def send_gates(step, i):
        return pltpu.make_async_remote_copy(
            src_ref=picked.at[step, lax.rem(d + i, 8)],
            dst_ref=gate_part.at[step, i - 1],
            send_sem=g_send.at[step, i - 1],
            recv_sem=g_recv.at[step, i - 1],
            device_id=row_to(i),
            device_id_type=MESH,
        )

    gate_row = z * 32 + iota((32, NSEC), 0)
    named = (gate_map[...] == gate_row).astype(jnp.bfloat16)
    col = iota((NSEC, 64), 1)
    section = 16 * (lax.rem(col // 16, 2) * 8 + lax.rem(d, 8)) + lax.rem(col, 16)
    chosen = (iota((NSEC, 64), 0) == section).astype(jnp.bfloat16)
    scale = 1.0 / math.sqrt(TMS * T_DEV / GATES)
    gate_hot = jnp.dot(named, chosen, preferred_element_type=jnp.float32)

    def route(step):
        for i in (1, 2, 3):
            send_z(step, i).wait_recv()
        gathered = row_sec[step].reshape(64, CHUNK * LANES) * scale
        gates = jnp.dot(gate_hot, gathered, precision=lax.Precision.HIGHEST)
        for k in range(8):
            picked[step, k] = gates[4 * k : 4 * k + 4]
        for i in range(1, 8):
            send_gates(step, i).start()

    def finish(step):
        total = picked[step, lax.rem(d, 8)]
        for i in range(1, 8):
            send_gates(step, i).wait_recv()
            total += gate_part[step, i - 1]
        out[:, step * CHUNK * LANES : (step + 1) * CHUNK * LANES] = total

    launch(0)
    for s in range(STEPS + 4):
        if s + 1 < STEPS:
            launch(s + 1)
        if s < STEPS:
            relay(s)
        if 1 <= s <= STEPS:
            settle(s - 1)
        if 2 <= s <= STEPS + 1:
            correlate(s - 2)
            for i in (1, 2, 3):
                send_z(s - 2, i).start()
        if 3 <= s <= STEPS + 2:
            route(s - 3)
        if 4 <= s:
            finish(s - 4)

    for step in range(STEPS):
        for way in range(2):
            send_far(step, way).wait_send()
            send_near(step, way).wait_send()
            send_edge(step, way).wait_send()
        for i in (1, 2, 3):
            send_z(step, i).wait_send()
        for i in range(1, 8):
            send_gates(step, i).wait_send()


def body(streams, beam_weights, code_signs, gate_map):
    dma = pltpu.SemaphoreType.DMA
    channels = streams.shape[1]
    tiles = streams.reshape(2, channels, GROUPS, LANES).transpose(1, 2, 0, 3)
    paired = beam_weights.transpose(1, 0, 2)
    f32, bf16, i16 = jnp.float32, jnp.bfloat16, jnp.int16
    vmem = pl.BlockSpec(memory_space=pltpu.VMEM)
    summed = pl.pallas_call(
        kernel,
        out_shape=jax.ShapeDtypeStruct((4, WIDE), f32),
        in_specs=[pl.BlockSpec(memory_space=pl.ANY), vmem, vmem, vmem],
        out_specs=vmem,
        scratch_shapes=[
            pltpu.VMEM((GROUPS, channels, 2, LANES), bf16),
            pltpu.VMEM((2, 200, WEIGHT_TILES * LANES), bf16),
            pltpu.VMEM((200, WEIGHT_TILES * BLOCK), bf16),
            pltpu.VMEM((100 * ROWS, LANES), f32),
            pltpu.VMEM((STEPS, 2, HALF + 16, LANES), i16),
            pltpu.VMEM((STEPS, PART + 16, LANES), i16),
            pltpu.VMEM((STEPS, PART + 16, LANES), i16),
            pltpu.VMEM((BEAMS * ROWS, LANES), bf16),
            pltpu.VMEM((BEAMS * ROWS, LANES), bf16),
            pltpu.VMEM((BEAMS * ROWS, LANES), bf16),
            pltpu.VMEM((256, LANES), bf16),
            pltpu.VMEM((256, LANES), bf16),
            pltpu.VMEM((32, LANES), f32),
            pltpu.VMEM((STEPS, 4, 16, CHUNK * LANES), f32),
            pltpu.VMEM((STEPS, 8, 4, CHUNK * LANES), f32),
            pltpu.VMEM((STEPS, 7, 4, CHUNK * LANES), f32),
            pltpu.VMEM((STEPS, 2, HALF + 16, LANES), i16),
            pltpu.VMEM((STEPS, 2, PART + 16, LANES), i16),
            dma((GROUPS,)),
            dma((STEPS, 2)), dma((STEPS, 2)), dma((STEPS, 2)), dma((STEPS, 2)),
            dma((STEPS, 2)), dma((STEPS, 2)),
            dma((STEPS, 3)), dma((STEPS, 3)), dma((STEPS, 7)), dma((STEPS, 7)),
        ],
        compiler_params=pltpu.CompilerParams(
            collective_id=0, has_side_effects=True, vmem_limit_bytes=48 * 2**20
        ),
    )(tiles, paired, code_signs, gate_map.reshape(1, NSEC))
    return summed.reshape(4, BEAMS, LANES)


def solution(mesh):
    placed = (P(None, "sub", "tm"), P(None, None, "sub"), P(), P())
    return jax.shard_map(
        body, mesh=mesh, in_specs=placed, out_specs=P("tm", "sub", None), check_vma=False
    )
```

```python
import functools
import math

import jax
import jax.numpy as jnp
from jax import lax
from jax.experimental import pallas as pl
from jax.experimental.pallas import tpu as pltpu
from jax.sharding import PartitionSpec as P

PKT = 32
IPP_LEN = 512
LAGS = 64
NCODES = 32
NBAUD = 16
BAUD_LEN = 8
SEC_LEN = 2
GATES = 128
NSEC = 256
LANES = 128
SUBS = 4
TMS = 32
BEAMS = 25
T_DEV = 4096
GROUPS = T_DEV // LANES
ROWS = 2 * GROUPS
PACKED = 16
SPAN = 4
WEIGHT_TILES = 5
CHUNK = 5
STEPS = BEAMS // CHUNK
LINES = 2 * CHUNK
PART = LINES * PACKED
HALF = PART // 2
BLOCK = 256
WIDE = BEAMS * LANES
BITS = 14.9
EARLY_RELAYS = ((), (0, 1), (2, 3), (4,))
EARLY_SETTLES = ((), (), (0,), (1, 2))
LATE_SETTLES = ((3,), (4,))
MESH = pl.DeviceIdType.MESH


def iota(shape, dim):
    return lax.broadcasted_iota(jnp.int32, shape, dim)


def kernel(
    streams, weights, code_signs, gate_map, out,
    held, plain, block_rows, sums, early, first, second, beams, signs,
    coded, skewed, row_sec, picked, gate_part, far_out, near_out,
    in_sem, a_send, a_recv, b_send, b_recv, h_send, h_recv, z_send, z_recv, g_send, g_recv,
):
    y = lax.axis_index("sub")
    d = lax.axis_index("tm")
    z = d // 8
    core = lax.rem(d, 2)
    based = lax.rem(d + TMS - 2 * core, TMS)

    def ring(step):
        return (y, lax.rem(d + step + TMS, TMS))

    def sub_to(step):
        return (lax.rem(y + step, SUBS), d)

    def z_to(step):
        return (y, lax.rem(z + step, 4) * 8 + lax.rem(d, 8))

    def row_to(step):
        return (y, z * 8 + lax.rem(d + step, 8))

    def fetch(i):
        return pltpu.make_async_copy(streams.at[:, i], held.at[i], in_sem.at[i])

    for i in range(GROUPS):
        fetch(i).start()

    barrier = pltpu.get_barrier_semaphore()
    met = [sub_to(1), sub_to(3), ring(-2), ring(2)]
    met += [z_to(i) for i in (1, 2, 3)] + [row_to(i) for i in range(1, 8)]
    for device in met:
        pl.semaphore_signal(barrier, inc=1, device_id=device, device_id_type=MESH)

    channels = weights.shape[2]
    stacked = weights[...].reshape(2 * weights.shape[0], channels)
    wide_rows = stacked.astype(jnp.float32)
    count = wide_rows.shape[0]
    odd = lax.rem(iota(wide_rows.shape, 0), 2) == 1
    turned_rows = jnp.where(odd, pltpu.roll(wide_rows, 1, 0), -pltpu.roll(wide_rows, count - 1, 0))
    plain[...] = jnp.zeros_like(plain)
    plain[0, :, 0:channels] = stacked
    plain[1, :, 0:channels] = turned_rows.astype(jnp.bfloat16)
    source = iota((BLOCK, BLOCK), 0)
    spread = (
        2 * lax.rem(source, LANES) + source // LANES == iota((BLOCK, BLOCK), 1)
    ).astype(jnp.bfloat16)
    for t in range(WEIGHT_TILES):
        cols = slice(t * LANES, (t + 1) * LANES)
        pair = jnp.concatenate([plain[0, :, cols], plain[1, :, cols]], 1)
        block_rows[:, t * BLOCK : (t + 1) * BLOCK] = jnp.dot(
            pair, spread, preferred_element_type=jnp.float32
        ).astype(jnp.bfloat16)
    samples = held.reshape(GROUPS, 2 * channels, LANES)

    def form(i, carry):
        for h in range(SPAN):
            fetch(SPAN * i + h).wait()
        product = jnp.dot(
            block_rows[:, 0 : 2 * channels],
            jnp.concatenate([samples[SPAN * i + h] for h in range(SPAN)], 1),
            preferred_element_type=jnp.float32,
        )
        for h in range(SPAN):
            place = SPAN * i + h
            sums[
                place // PACKED, pl.ds(lax.rem(place, PACKED), count, stride=PACKED), :
            ] = product[:, h * LANES : (h + 1) * LANES]
        top = jnp.max(jnp.abs(product).reshape(count // 8, 8, SPAN * LANES), axis=0)
        return jnp.maximum(carry, top)

    nothing = jnp.zeros((8, SPAN * LANES), jnp.float32)
    blocks = GROUPS // SPAN

    def level_of(top):
        most = jnp.maximum(jnp.max(top, axis=(0, 1), keepdims=True), 1e-30)
        return jnp.broadcast_to(jnp.ceil(jnp.log2(most)), (PACKED, LANES))

    def rows_of(owner, step):
        return pl.multiple_of((owner * BEAMS + step * CHUNK) * 2 * PACKED, PACKED)

    def packed(value, power):
        steps = value.reshape(-1, 16, LANES) * jnp.exp2(BITS - power)[None]
        return jnp.round(steps).astype(jnp.int32).astype(jnp.int16).reshape(-1, LANES)

    def unpacked(ref, count):
        power = ref[count : count + 16, :].astype(jnp.int32).astype(jnp.float32)
        steps = ref[0:count, :].astype(jnp.int32).astype(jnp.float32)
        value = steps.reshape(-1, 16, LANES) * jnp.exp2(power - BITS)[None]
        return value.reshape(count, LANES), power

    def ways(way):
        return 1 if way == 0 else 3

    def send_far(t, step, way):
        return pltpu.make_async_remote_copy(
            src_ref=far_out.at[t, step, way],
            dst_ref=early.at[t, step, way],
            send_sem=a_send.at[t, step, way],
            recv_sem=a_recv.at[t, step, way],
            device_id=sub_to(ways(way)),
            device_id_type=MESH,
        )

    def send_near(t, step, way):
        landing = first if way == 0 else second
        return pltpu.make_async_remote_copy(
            src_ref=near_out.at[t, step, way],
            dst_ref=landing.at[t, step],
            send_sem=b_send.at[t, step, way],
            recv_sem=b_recv.at[t, step, way],
            device_id=sub_to(ways(way)),
            device_id_type=MESH,
        )

    def launch(t, step):
        for way in range(2):
            start = rows_of(lax.rem(y + 2, SUBS), step) + way * HALF
            far_out[t, step, way, 0:HALF, :] = packed(sums[t, pl.ds(start, HALF), :], level[t])
            far_out[t, step, way, HALF : HALF + 16, :] = (
                level[t].astype(jnp.int32).astype(jnp.int16)
            )
            send_far(t, step, way).start()

    def send_edge(step, way):
        lines = pl.ds(step * LINES, LINES)
        return pltpu.make_async_remote_copy(
            src_ref=beams.at[2 * core, lines],
            dst_ref=beams.at[1 if way == 0 else 2 - 2 * core, lines],
            send_sem=h_send.at[step, way],
            recv_sem=h_recv.at[step, way],
            device_id=(y, d + 1 - 2 * core) if way == 0 else ring(4 * core - 2),
            device_id_type=MESH,
        )

    row = iota((256, NCODES), 0)
    code_of = lax.rem(
        2 * lax.rem(4 * lax.rem(row, GROUPS) + row // 64, 16) + based // 16, NCODES
    )
    code_hot = (code_of == iota((256, NCODES), 1)).astype(jnp.bfloat16)
    lane16 = iota((NBAUD, LANES), 1)
    baud_hot = jnp.where(
        (lax.rem(4 * based + lane16 // BAUD_LEN, NBAUD) == iota((NBAUD, LANES), 0)) & (lane16 < 96),
        1.0,
        0.0,
    ).astype(jnp.bfloat16)
    table = (2 * code_signs[...] - 1).astype(jnp.float32).astype(jnp.bfloat16)
    by_code = jnp.dot(code_hot, table, preferred_element_type=jnp.float32).astype(jnp.bfloat16)
    signs[...] = jnp.dot(by_code, baud_hot, preferred_element_type=jnp.float32).astype(jnp.bfloat16)

    def relay(t, step):
        for way in range(2):
            send_far(t, step, way).wait_recv()
            start = rows_of(lax.rem(y + ways(way), SUBS), step)
            passed, power = unpacked(early.at[t, step, way], HALF)
            both = jnp.maximum(power, level[t]) + 1
            mine = slice(way * HALF, (way + 1) * HALF)
            rest = slice((1 - way) * HALF, (2 - way) * HALF)
            near_out[t, step, way, mine, :] = packed(
                sums[t, pl.ds(start + way * HALF, HALF), :] + passed, both
            )
            near_out[t, step, way, rest, :] = packed(
                sums[t, pl.ds(start + (1 - way) * HALF, HALF), :], both
            )
            near_out[t, step, way, PART : PART + 16, :] = both.astype(jnp.int32).astype(jnp.int16)
            send_near(t, step, way).start()

    def settle(t, step):
        for way in range(2):
            send_near(t, step, way).wait_recv()
        total = sums[t, pl.ds(rows_of(y, step), PART), :]
        total += unpacked(first.at[t, step], PART)[0] + unpacked(second.at[t, step], PART)[0]
        beams[2 * core, step * LINES : (step + 1) * LINES, t] = total.astype(jnp.bfloat16).reshape(
            LINES, PACKED, LANES
        )

    def share(step):
        for way in range(2):
            send_edge(step, way).start()

    span = CHUNK * ROWS
    lane = iota((span, LANES), 1)
    offset = iota((span, LANES), 0)

    def passed_end(slot, step):
        lines = slice(step * LINES, (step + 1) * LINES)
        turned = pltpu.roll(beams[slot, lines].reshape(span, LANES).astype(jnp.float32), 96, 1)
        above = pltpu.roll(turned, span - 1, 0)
        last = lax.rem(offset, GROUPS) == GROUPS - 1
        new = jnp.where(lane < 96, turned, jnp.where(last, 0.0, above))
        beams[slot, lines] = new.astype(jnp.bfloat16).reshape(LINES, 2, PACKED, LANES)

    def correlate(step):
        for way in range(2):
            send_edge(step, way).wait()

        @pl.when(d == 1)
        def _():
            passed_end(1, step)

        @pl.when((d == 1) | (d == TMS - 2))
        def _():
            passed_end(2, step)

        lines = slice(step * LINES, (step + 1) * LINES)
        three = [beams[slot, lines].reshape(span, LANES) for slot in range(3)]
        for c in range(4):
            here, n1, n2 = [
                pltpu.roll(v, shift, 1) if shift else v
                for v, shift in ((v, (128 + 32 * (j - c)) % 128) for j, v in enumerate(three))
            ]
            mixed = jnp.where(lane < 32, here, jnp.where(lane < 64, n1, n2))
            mixed = mixed.reshape(CHUNK, ROWS, LANES) * signs[c * ROWS : (c + 1) * ROWS, :][None]
            coded[:, :, c] = mixed.reshape(CHUNK, 2, GROUPS, LANES)
        grams = []
        low = iota((256, LANES), 1) < 32
        for k in range(CHUNK):
            later = coded[k].reshape(256, LANES)
            turned = jnp.concatenate([-later[128:], later[:128]], 0)
            base = jnp.where(low, later, pltpu.roll(turned, 32, 1))
            gram = lax.dot_general(
                base, later, (((0,), (0,)), ((), ())), preferred_element_type=jnp.float32
            )
            real = jnp.concatenate(
                [pltpu.roll(gram[r : r + 8], 127 - r, 1) for r in (0, 8, 16, 24)], 0
            )
            imag = jnp.concatenate(
                [pltpu.roll(gram[r + 32 : r + 40], (191 - r) % 128, 1) for r in (0, 8, 16, 24)], 0
            )
            grams += [real, imag]
        gram = jnp.concatenate(grams, 0)
        for bit in (1, 2, 4):
            gram = jnp.where((offset & bit) > 0, pltpu.roll(gram, LANES - bit, 1), gram)
        gram = gram.reshape(CHUNK, 2, 32, LANES)
        skewed[...] = jnp.where(iota((CHUNK, 32, LANES), 2) < LAGS, gram[:, 0], gram[:, 1]).reshape(
            CHUNK * 32, LANES
        )
        pairs = skewed[pl.ds(0, CHUNK * 16, stride=2), :] + skewed[pl.ds(1, CHUNK * 16, stride=2), :]
        for k in range(CHUNK):
            row_sec[step, z, :, k * LANES : (k + 1) * LANES] = pairs[16 * k : 16 * k + 16]

    def send_z(step, i):
        return pltpu.make_async_remote_copy(
            src_ref=row_sec.at[step, z],
            dst_ref=row_sec.at[step, z],
            send_sem=z_send.at[step, i - 1],
            recv_sem=z_recv.at[step, i - 1],
            device_id=z_to(i),
            device_id_type=MESH,
        )

    def send_gates(step, i):
        return pltpu.make_async_remote_copy(
            src_ref=picked.at[step, lax.rem(d + i, 8)],
            dst_ref=gate_part.at[step, i - 1],
            send_sem=g_send.at[step, i - 1],
            recv_sem=g_recv.at[step, i - 1],
            device_id=row_to(i),
            device_id_type=MESH,
        )

    gate_row = z * 32 + iota((32, NSEC), 0)
    named = (gate_map[...] == gate_row).astype(jnp.bfloat16)
    col = iota((NSEC, 64), 1)
    origin = lax.rem(col // 16 * 8 + lax.rem(d, 8) + TMS - 2 * core, 16)
    section = 16 * origin + lax.rem(col, 16)
    chosen = (iota((NSEC, 64), 0) == section).astype(jnp.bfloat16)
    scale = 1.0 / math.sqrt(TMS * T_DEV / GATES)
    gate_hot = jnp.dot(named, chosen, preferred_element_type=jnp.float32)

    def route(step):
        for i in (1, 2, 3):
            send_z(step, i).wait_recv()
        gathered = row_sec[step].reshape(64, CHUNK * LANES) * scale
        gates = jnp.dot(gate_hot, gathered, precision=lax.Precision.HIGHEST)
        for k in range(8):
            picked[step, k] = gates[4 * k : 4 * k + 4]
        for i in range(1, 8):
            send_gates(step, i).start()

    def finish(step):
        total = picked[step, lax.rem(d, 8)]
        for i in range(1, 8):
            send_gates(step, i).wait_recv()
            total += gate_part[step, i - 1]
        out[:, step * CHUNK * LANES : (step + 1) * CHUNK * LANES] = total

    level = [None, None]
    level[0] = level_of(lax.fori_loop(0, blocks // 2, form, nothing))
    pl.semaphore_wait(barrier, len(met))
    for j in range(STEPS):
        launch(0, j)
    top = nothing
    for i in range(blocks // 2):
        top = form(blocks // 2 + i, top)
        for j in EARLY_RELAYS[i]:
            relay(0, j)
        for j in EARLY_SETTLES[i]:
            settle(0, j)
    level[1] = level_of(top)
    launch(1, 0)
    for s in range(STEPS + 4):
        if s + 1 < STEPS:
            launch(1, s + 1)
        if s < STEPS:
            relay(1, s)
        for j in LATE_SETTLES[s] if s < len(LATE_SETTLES) else ():
            settle(0, j)
        if 1 <= s <= STEPS:
            settle(1, s - 1)
            share(s - 1)
        if 2 <= s <= STEPS + 1:
            correlate(s - 2)
            for i in (1, 2, 3):
                send_z(s - 2, i).start()
        if 3 <= s <= STEPS + 2:
            route(s - 3)
        if 4 <= s:
            finish(s - 4)

    for step in range(STEPS):
        for t in range(2):
            for way in range(2):
                send_far(t, step, way).wait_send()
                send_near(t, step, way).wait_send()
        for i in (1, 2, 3):
            send_z(step, i).wait_send()
        for i in range(1, 8):
            send_gates(step, i).wait_send()


def body(streams, beam_weights, code_signs, gate_map):
    dma = pltpu.SemaphoreType.DMA
    channels = streams.shape[1]
    tiles = streams.reshape(2, channels, GROUPS, LANES).transpose(1, 2, 0, 3)
    paired = beam_weights.transpose(1, 0, 2)
    f32, bf16, i16 = jnp.float32, jnp.bfloat16, jnp.int16
    vmem = pl.BlockSpec(memory_space=pltpu.VMEM)
    summed = pl.pallas_call(
        kernel,
        out_shape=jax.ShapeDtypeStruct((4, WIDE), f32),
        in_specs=[pl.BlockSpec(memory_space=pl.ANY), vmem, vmem, vmem],
        out_specs=vmem,
        scratch_shapes=[
            pltpu.VMEM((GROUPS, channels, 2, LANES), bf16),
            pltpu.VMEM((2, 200, WEIGHT_TILES * LANES), bf16),
            pltpu.VMEM((200, WEIGHT_TILES * BLOCK), bf16),
            pltpu.VMEM((2, 200 * PACKED, LANES), f32),
            pltpu.VMEM((2, STEPS, 2, HALF + 16, LANES), i16),
            pltpu.VMEM((2, STEPS, PART + 16, LANES), i16),
            pltpu.VMEM((2, STEPS, PART + 16, LANES), i16),
            pltpu.VMEM((3, 2 * BEAMS, 2, PACKED, LANES), bf16),
            pltpu.VMEM((256, LANES), bf16),
            pltpu.VMEM((CHUNK, 2, 4, GROUPS, LANES), bf16),
            pltpu.VMEM((CHUNK * 32, LANES), f32),
            pltpu.VMEM((STEPS, 4, 16, CHUNK * LANES), f32),
            pltpu.VMEM((STEPS, 8, 4, CHUNK * LANES), f32),
            pltpu.VMEM((STEPS, 7, 4, CHUNK * LANES), f32),
            pltpu.VMEM((2, STEPS, 2, HALF + 16, LANES), i16),
            pltpu.VMEM((2, STEPS, 2, PART + 16, LANES), i16),
            dma((GROUPS,)),
            dma((2, STEPS, 2)), dma((2, STEPS, 2)), dma((2, STEPS, 2)), dma((2, STEPS, 2)),
            dma((STEPS, 2)), dma((STEPS, 2)),
            dma((STEPS, 3)), dma((STEPS, 3)), dma((STEPS, 7)), dma((STEPS, 7)),
        ],
        compiler_params=pltpu.CompilerParams(
            collective_id=0, has_side_effects=True, vmem_limit_bytes=48 * 2**20
        ),
    )(tiles, paired, code_signs, gate_map.reshape(1, NSEC))
    return summed.reshape(4, BEAMS, LANES)


def solution(mesh):
    placed = (P(None, "sub", "tm"), P(None, None, "sub"), P(), P())
    return jax.shard_map(
        body, mesh=mesh, in_specs=placed, out_specs=P("tm", "sub", None), check_vma=False
    )
```

```python
import functools
import math

import jax
import jax.numpy as jnp
from jax import lax
from jax.experimental import pallas as pl
from jax.experimental.pallas import tpu as pltpu
from jax.sharding import PartitionSpec as P

PKT = 32
IPP_LEN = 512
LAGS = 64
NCODES = 32
NBAUD = 16
BAUD_LEN = 8
SEC_LEN = 2
GATES = 128
NSEC = 256
LANES = 128
SUBS = 4
TMS = 32
BEAMS = 25
T_DEV = 4096
GROUPS = T_DEV // LANES
ROWS = 2 * GROUPS
SPAN = 4
WEIGHT_TILES = 5
SIZES = (6, 6, 5, 4, 4)
STARTS = (0, 6, 12, 17, 21)
STEPS = len(SIZES)
MOST = max(SIZES)
BLOCK = 256
WIDE = BEAMS * LANES
BITS = 14.9
AHEAD = 2
LAG_PAIR = 4
LAG_ROUTE = 8
MESH = pl.DeviceIdType.MESH


def iota(shape, dim):
    return lax.broadcasted_iota(jnp.int32, shape, dim)


def kernel(
    streams, weights, code_signs, gate_map, out,
    held, raw_weights, raw_gates, plain, block_rows, sums, early, late, beams, signs,
    coded, skewed, row_sec, picked, gate_part, far_out, near_out,
    in_sem, w_sem, a_send, a_recv, b_send, b_recv, h_send, h_recv, z_send, z_recv, g_send, g_recv,
):
    y = lax.axis_index("sub")
    d = lax.axis_index("tm")
    z = d // 8
    core = lax.rem(d, 2)
    based = lax.rem(d + TMS - 2 * core, TMS)

    def ring(step):
        return (y, lax.rem(d + step + TMS, TMS))

    def sub_to(step):
        return (lax.rem(y + step, SUBS), d)

    def z_to(step):
        return (y, lax.rem(z + step, 4) * 8 + lax.rem(d, 8))

    def row_to(step):
        return (y, z * 8 + lax.rem(d + step, 8))

    def fetch(i):
        return pltpu.make_async_copy(streams.at[:, i], held.at[i], in_sem.at[i])

    fetch_weights = pltpu.make_async_copy(weights, raw_weights, w_sem.at[0])
    fetch_gates = pltpu.make_async_copy(gate_map, raw_gates, w_sem.at[1])
    fetch_weights.start()
    for i in range(GROUPS):
        fetch(i).start()
    fetch_gates.start()

    barrier = pltpu.get_barrier_semaphore()
    met = [sub_to(1), sub_to(3), ring(-2), ring(2)]
    met += [z_to(i) for i in (1, 2, 3)] + [row_to(i) for i in range(1, 8)]
    for device in met:
        pl.semaphore_signal(barrier, inc=1, device_id=device, device_id_type=MESH)

    channels = weights.shape[2]
    fetch_weights.wait()
    stacked = raw_weights[...].reshape(2 * weights.shape[0], channels)
    wide_rows = stacked.astype(jnp.float32)
    count = wide_rows.shape[0]
    odd = lax.rem(iota(wide_rows.shape, 0), 2) == 1
    turned_rows = jnp.where(odd, pltpu.roll(wide_rows, 1, 0), -pltpu.roll(wide_rows, count - 1, 0))
    plain[...] = jnp.zeros_like(plain)
    plain[0, :, 0:channels] = stacked
    plain[1, :, 0:channels] = turned_rows.astype(jnp.bfloat16)
    source = iota((BLOCK, BLOCK), 0)
    spread = (
        2 * lax.rem(source, LANES) + source // LANES == iota((BLOCK, BLOCK), 1)
    ).astype(jnp.bfloat16)
    for t in range(WEIGHT_TILES):
        cols = slice(t * LANES, (t + 1) * LANES)
        pair = jnp.concatenate([plain[0, :, cols], plain[1, :, cols]], 1)
        block_rows[:, t * BLOCK : (t + 1) * BLOCK] = jnp.dot(
            pair, spread, preferred_element_type=jnp.float32
        ).astype(jnp.bfloat16)
    samples = held.reshape(GROUPS, 2 * channels, LANES)

    def form(i, carry):
        for h in range(SPAN):
            fetch(SPAN * i + h).wait()
        product = jnp.dot(
            block_rows[:, 0 : 2 * channels],
            jnp.concatenate([samples[SPAN * i + h] for h in range(SPAN)], 1),
            preferred_element_type=jnp.float32,
        )
        for h in range(SPAN):
            place = SPAN * i + h
            sums[pl.ds(place, count, stride=GROUPS), :] = product[:, h * LANES : (h + 1) * LANES]
        top = jnp.max(jnp.abs(product).reshape(count // 8, 8, SPAN * LANES), axis=0)
        return jnp.maximum(carry, top)

    nothing = jnp.zeros((8, SPAN * LANES), jnp.float32)
    blocks = GROUPS // SPAN

    def level_of(top):
        most = jnp.maximum(jnp.max(top, axis=(0, 1), keepdims=True), 1e-30)
        return jnp.broadcast_to(jnp.ceil(jnp.log2(most)), (16, LANES))

    def rows_of(owner, step):
        return pl.multiple_of((owner * BEAMS + STARTS[step]) * ROWS, ROWS)

    def packed(value, power):
        steps = value.reshape(-1, 16, LANES) * jnp.exp2(BITS - power)[None]
        return jnp.round(steps).astype(jnp.int32).astype(jnp.int16).reshape(-1, LANES)

    def unpacked(ref, count):
        power = ref[count : count + 16, :].astype(jnp.int32).astype(jnp.float32)
        steps = ref[0:count, :].astype(jnp.int32).astype(jnp.float32)
        value = steps.reshape(-1, 16, LANES) * jnp.exp2(power - BITS)[None]
        return value.reshape(count, LANES), power

    def ways(way):
        return 1 if way == 0 else 3

    def send_far(step, way):
        half = SIZES[step] * GROUPS
        rows = pl.ds(STARTS[step] * GROUPS + 16 * step, half + 16)
        return pltpu.make_async_remote_copy(
            src_ref=far_out.at[way, rows],
            dst_ref=early.at[way, rows],
            send_sem=a_send.at[step, way],
            recv_sem=a_recv.at[step, way],
            device_id=sub_to(ways(way)),
            device_id_type=MESH,
        )

    def near_rows(step):
        return pl.ds(STARTS[step] * ROWS + 16 * step, SIZES[step] * ROWS + 16)

    def send_near(step, way):
        rows = near_rows(step)
        return pltpu.make_async_remote_copy(
            src_ref=near_out.at[way, rows],
            dst_ref=late.at[way, rows],
            send_sem=b_send.at[step, way],
            recv_sem=b_recv.at[step, way],
            device_id=sub_to(ways(way)),
            device_id_type=MESH,
        )

    def launch(step):
        half = SIZES[step] * GROUPS
        place = STARTS[step] * GROUPS + 16 * step
        for way in range(2):
            start = rows_of(lax.rem(y + 2, SUBS), step) + way * half
            far_out[way, place : place + half, :] = packed(sums[pl.ds(start, half), :], level)
            far_out[way, place + half : place + half + 16, :] = (
                level.astype(jnp.int32).astype(jnp.int16)
            )
            send_far(step, way).start()

    def send_edge(step, way):
        lines = pl.ds(2 * STARTS[step], 2 * SIZES[step])
        return pltpu.make_async_remote_copy(
            src_ref=beams.at[2 * core, lines],
            dst_ref=beams.at[1 if way == 0 else 2 - 2 * core, lines],
            send_sem=h_send.at[step, way],
            recv_sem=h_recv.at[step, way],
            device_id=(y, d + 1 - 2 * core) if way == 0 else ring(4 * core - 2),
            device_id_type=MESH,
        )

    row = iota((256, NCODES), 0)
    code_of = lax.rem(
        2 * lax.rem(4 * lax.rem(row, GROUPS) + row // 64, 16) + based // 16, NCODES
    )
    code_hot = (code_of == iota((256, NCODES), 1)).astype(jnp.bfloat16)
    lane16 = iota((NBAUD, LANES), 1)
    baud_hot = jnp.where(
        (lax.rem(4 * based + lane16 // BAUD_LEN, NBAUD) == iota((NBAUD, LANES), 0)) & (lane16 < 96),
        1.0,
        0.0,
    ).astype(jnp.bfloat16)
    table = (2 * code_signs[...] - 1).astype(jnp.float32).astype(jnp.bfloat16)
    by_code = lax.dot_general(
        code_hot, table, (((1,), (1,)), ((), ())), preferred_element_type=jnp.float32
    ).astype(jnp.bfloat16)
    signs[...] = jnp.dot(by_code, baud_hot, preferred_element_type=jnp.float32).astype(jnp.bfloat16)

    def relay(step):
        half = SIZES[step] * GROUPS
        place = STARTS[step] * GROUPS + 16 * step
        spot = STARTS[step] * ROWS + 16 * step
        for way in range(2):
            send_far(step, way).wait_recv()
            start = rows_of(lax.rem(y + ways(way), SUBS), step)
            passed, power = unpacked(early.at[way, pl.ds(place, half + 16)], half)
            both = jnp.maximum(power, level) + 1
            mine, rest = way * half, (1 - way) * half
            near_out[way, spot + mine : spot + mine + half, :] = packed(
                sums[pl.ds(start + mine, half), :] + passed, both
            )
            near_out[way, spot + rest : spot + rest + half, :] = packed(
                sums[pl.ds(start + rest, half), :], both
            )
            near_out[way, spot + 2 * half : spot + 2 * half + 16, :] = (
                both.astype(jnp.int32).astype(jnp.int16)
            )
            send_near(step, way).start()

    def settle(step):
        part = SIZES[step] * ROWS
        total = sums[pl.ds(rows_of(y, step), part), :]
        for way in range(2):
            send_near(step, way).wait_recv()
            total += unpacked(late.at[way, near_rows(step)], part)[0]
        beams[2 * core, 2 * STARTS[step] : 2 * (STARTS[step] + SIZES[step])] = total.astype(
            jnp.bfloat16
        ).reshape(2 * SIZES[step], GROUPS, LANES)

    def share(step):
        for way in range(2):
            send_edge(step, way).start()

    def passed_end(slot, step):
        span = SIZES[step] * ROWS
        lines = slice(2 * STARTS[step], 2 * (STARTS[step] + SIZES[step]))
        turned = pltpu.roll(beams[slot, lines].reshape(span, LANES).astype(jnp.float32), 96, 1)
        above = pltpu.roll(turned, span - 1, 0)
        last = lax.rem(iota((span, LANES), 0), GROUPS) == GROUPS - 1
        new = jnp.where(iota((span, LANES), 1) < 96, turned, jnp.where(last, 0.0, above))
        beams[slot, lines] = new.astype(jnp.bfloat16).reshape(2 * SIZES[step], GROUPS, LANES)

    def correlate(step):
        for way in range(2):
            send_edge(step, way).wait()

        @pl.when(d == 1)
        def _():
            passed_end(1, step)

        @pl.when((d == 1) | (d == TMS - 2))
        def _():
            passed_end(2, step)

        size = SIZES[step]
        span = size * ROWS
        lane = iota((span, LANES), 1)
        offset = iota((span, LANES), 0)
        lines = slice(2 * STARTS[step], 2 * (STARTS[step] + size))
        three = [beams[slot, lines].reshape(span, LANES) for slot in range(3)]
        for c in range(4):
            here, n1, n2 = [
                pltpu.roll(v, shift, 1) if shift else v
                for v, shift in ((v, (128 + 32 * (j - c)) % 128) for j, v in enumerate(three))
            ]
            mixed = jnp.where(lane < 32, here, jnp.where(lane < 64, n1, n2))
            mixed = mixed.reshape(size, ROWS, LANES) * signs[c * ROWS : (c + 1) * ROWS, :][None]
            coded[0:size, :, c] = mixed.reshape(size, 2, GROUPS, LANES)
        grams = []
        low = iota((256, LANES), 1) < 32
        for k in range(size):
            later = coded[k].reshape(256, LANES)
            turned = jnp.concatenate([-later[128:], later[:128]], 0)
            base = jnp.where(low, later, pltpu.roll(turned, 32, 1))
            gram = lax.dot_general(
                base, later, (((0,), (0,)), ((), ())), preferred_element_type=jnp.float32
            )
            real = jnp.concatenate(
                [pltpu.roll(gram[r : r + 8], 127 - r, 1) for r in (0, 8, 16, 24)], 0
            )
            imag = jnp.concatenate(
                [pltpu.roll(gram[r + 32 : r + 40], (191 - r) % 128, 1) for r in (0, 8, 16, 24)], 0
            )
            grams += [real, imag]
        gram = jnp.concatenate(grams, 0)
        for bit in (1, 2, 4):
            gram = jnp.where((offset & bit) > 0, pltpu.roll(gram, LANES - bit, 1), gram)
        gram = gram.reshape(size, 2, 32, LANES)
        skewed[0 : size * 32] = jnp.where(
            iota((size, 32, LANES), 2) < LAGS, gram[:, 0], gram[:, 1]
        ).reshape(size * 32, LANES)
        even = skewed[pl.ds(0, size * 16, stride=2), :]
        pairs = even + skewed[pl.ds(1, size * 16, stride=2), :]
        for k in range(size):
            place = (STARTS[step] + k) * LANES
            row_sec[z, :, place : place + LANES] = pairs[16 * k : 16 * k + 16].astype(
                jnp.bfloat16
            )

    def cols_of(step):
        return pl.ds(STARTS[step] * LANES, SIZES[step] * LANES)

    def send_z(step, i):
        return pltpu.make_async_remote_copy(
            src_ref=row_sec.at[z, :, cols_of(step)],
            dst_ref=row_sec.at[z, :, cols_of(step)],
            send_sem=z_send.at[step, i - 1],
            recv_sem=z_recv.at[step, i - 1],
            device_id=z_to(i),
            device_id_type=MESH,
        )

    def send_gates(step, i):
        return pltpu.make_async_remote_copy(
            src_ref=picked.at[lax.rem(d + i, 8), :, cols_of(step)],
            dst_ref=gate_part.at[i - 1, :, cols_of(step)],
            send_sem=g_send.at[step, i - 1],
            recv_sem=g_recv.at[step, i - 1],
            device_id=row_to(i),
            device_id_type=MESH,
        )

    fetch_gates.wait()
    gate_row = z * 32 + iota((32, NSEC), 0)
    named = (raw_gates[...] == gate_row).astype(jnp.bfloat16)
    col = iota((NSEC, 64), 1)
    origin = lax.rem(col // 16 * 8 + lax.rem(d, 8) + TMS - 2 * core, 16)
    section = 16 * origin + lax.rem(col, 16)
    chosen = (iota((NSEC, 64), 0) == section).astype(jnp.bfloat16)
    scale = 1.0 / math.sqrt(TMS * T_DEV / GATES)
    gate_hot = jnp.dot(named, chosen, preferred_element_type=jnp.float32).astype(jnp.bfloat16)

    def route(step):
        for i in (1, 2, 3):
            send_z(step, i).wait_recv()
        gathered = row_sec[:, :, cols_of(step)].reshape(64, SIZES[step] * LANES)
        gates = jnp.dot(gate_hot, gathered, preferred_element_type=jnp.float32) * scale
        for k in range(8):
            picked[k, :, cols_of(step)] = gates[4 * k : 4 * k + 4]
        for i in range(1, 8):
            send_gates(step, i).start()

    def finish(step):
        total = picked[lax.rem(d, 8), :, cols_of(step)]
        for i in range(1, 8):
            send_gates(step, i).wait_recv()
            total += gate_part[i - 1, :, cols_of(step)]
        out[:, cols_of(step)] = total

    level = level_of(lax.fori_loop(0, blocks, form, nothing))
    pl.semaphore_wait(barrier, len(met))
    for s in range(AHEAD):
        launch(s)
    for s in range(STEPS + LAG_ROUTE):
        if s + AHEAD < STEPS:
            launch(s + AHEAD)
        if s < STEPS:
            relay(s)
        if 1 <= s <= STEPS:
            settle(s - 1)
            share(s - 1)
        if 0 <= s - LAG_PAIR < STEPS:
            correlate(s - LAG_PAIR)
            for i in (1, 2, 3):
                send_z(s - LAG_PAIR, i).start()
        if 0 <= s - LAG_ROUTE:
            route(s - LAG_ROUTE)
    for step in range(STEPS):
        finish(step)

    for step in range(STEPS):
        for way in range(2):
            send_far(step, way).wait_send()
            send_near(step, way).wait_send()
        for i in (1, 2, 3):
            send_z(step, i).wait_send()
        for i in range(1, 8):
            send_gates(step, i).wait_send()


def body(streams, beam_weights, code_signs, gate_map):
    dma = pltpu.SemaphoreType.DMA
    channels = streams.shape[1]
    tiles = streams.reshape(2, channels, GROUPS, LANES).transpose(1, 2, 0, 3)
    paired = beam_weights.transpose(1, 0, 2)
    f32, bf16, i16 = jnp.float32, jnp.bfloat16, jnp.int16
    vmem = pl.BlockSpec(memory_space=pltpu.VMEM)
    hbm = pl.BlockSpec(memory_space=pltpu.HBM)
    summed = pl.pallas_call(
        kernel,
        out_shape=jax.ShapeDtypeStruct((4, WIDE), f32),
        in_specs=[hbm, hbm, vmem, hbm],
        out_specs=vmem,
        scratch_shapes=[
            pltpu.VMEM((GROUPS, channels, 2, LANES), bf16),
            pltpu.VMEM((100, 2, channels), bf16),
            pltpu.VMEM((1, NSEC), jnp.int32),
            pltpu.VMEM((2, 200, WEIGHT_TILES * LANES), bf16),
            pltpu.VMEM((200, WEIGHT_TILES * BLOCK), bf16),
            pltpu.VMEM((100 * ROWS, LANES), f32),
            pltpu.VMEM((2, BEAMS * GROUPS + 16 * STEPS, LANES), i16),
            pltpu.VMEM((2, BEAMS * ROWS + 16 * STEPS, LANES), i16),
            pltpu.VMEM((3, 2 * BEAMS, GROUPS, LANES), bf16),
            pltpu.VMEM((256, LANES), bf16),
            pltpu.VMEM((MOST, 2, 4, GROUPS, LANES), bf16),
            pltpu.VMEM((MOST * 32, LANES), f32),
            pltpu.VMEM((4, 16, WIDE), bf16),
            pltpu.VMEM((8, 4, WIDE), f32),
            pltpu.VMEM((7, 4, WIDE), f32),
            pltpu.VMEM((2, BEAMS * GROUPS + 16 * STEPS, LANES), i16),
            pltpu.VMEM((2, BEAMS * ROWS + 16 * STEPS, LANES), i16),
            dma((GROUPS,)), dma((2,)),
            dma((STEPS, 2)), dma((STEPS, 2)), dma((STEPS, 2)), dma((STEPS, 2)),
            dma((STEPS, 2)), dma((STEPS, 2)),
            dma((STEPS, 3)), dma((STEPS, 3)), dma((STEPS, 7)), dma((STEPS, 7)),
        ],
        compiler_params=pltpu.CompilerParams(
            collective_id=0, has_side_effects=True, vmem_limit_bytes=48 * 2**20
        ),
    )(tiles, paired, code_signs.T, gate_map.reshape(1, NSEC))
    return summed.reshape(4, BEAMS, LANES)


def solution(mesh):
    placed = (P(None, "sub", "tm"), P(None, None, "sub"), P(), P())
    return jax.shard_map(
        body, mesh=mesh, in_specs=placed, out_specs=P("tm", "sub", None), check_vma=False
    )
```

```python
import functools
import math

import jax
import jax.numpy as jnp
from jax import lax
from jax.experimental import pallas as pl
from jax.experimental.pallas import tpu as pltpu
from jax.sharding import PartitionSpec as P

PKT = 32
IPP_LEN = 512
LAGS = 64
NCODES = 32
NBAUD = 16
BAUD_LEN = 8
SEC_LEN = 2
GATES = 128
NSEC = 256
LANES = 128
SUBS = 4
TMS = 32
BEAMS = 25
T_DEV = 4096
GROUPS = T_DEV // LANES
ROWS = 2 * GROUPS
SPAN = 4
WEIGHT_TILES = 5
SIZES = (6, 6, 5, 4, 4)
STARTS = (0, 6, 12, 17, 21)
STEPS = len(SIZES)
MOST = max(SIZES)
BLOCK = 256
WIDE = BEAMS * LANES
BITS = 14.9
AHEAD = 2
LAG_PAIR = 4
LAG_ROUTE = 8
MESH = pl.DeviceIdType.MESH


def iota(shape, dim):
    return lax.broadcasted_iota(jnp.int32, shape, dim)


def kernel(
    streams, weights, code_signs, gate_map, out,
    held, raw_weights, raw_gates, plain, block_rows, sums, early, late, beams, signs,
    coded, skewed, row_sec, picked, gate_part, far_out, near_out,
    in_sem, w_sem, a_send, a_recv, b_send, b_recv, h_send, h_recv, z_send, z_recv, g_send, g_recv,
):
    y = lax.axis_index("sub")
    d = lax.axis_index("tm")
    z = d // 8
    core = lax.rem(d, 2)
    based = lax.rem(d + TMS - 2 * core, TMS)

    def ring(step):
        return (y, lax.rem(d + step + TMS, TMS))

    def sub_to(step):
        return (lax.rem(y + step, SUBS), d)

    def z_to(step):
        return (y, lax.rem(z + step, 4) * 8 + lax.rem(d, 8))

    def row_to(step):
        return (y, z * 8 + lax.rem(d + step, 8))

    def fetch(i):
        return pltpu.make_async_copy(streams.at[:, i], held.at[i], in_sem.at[i])

    fetch_weights = pltpu.make_async_copy(weights, raw_weights, w_sem.at[0])
    fetch_gates = pltpu.make_async_copy(gate_map, raw_gates, w_sem.at[1])
    fetch_weights.start()
    for i in range(GROUPS):
        fetch(i).start()
    fetch_gates.start()

    barrier = pltpu.get_barrier_semaphore()
    met = [sub_to(1), sub_to(3), ring(-2), ring(2)]
    met += [z_to(i) for i in (1, 2, 3)] + [row_to(i) for i in range(1, 8)]
    for device in met:
        pl.semaphore_signal(barrier, inc=1, device_id=device, device_id_type=MESH)

    channels = weights.shape[2]
    fetch_weights.wait()
    stacked = raw_weights[...].reshape(2 * weights.shape[0], channels)
    wide_rows = stacked.astype(jnp.float32)
    count = wide_rows.shape[0]
    odd = lax.rem(iota(wide_rows.shape, 0), 2) == 1
    turned_rows = jnp.where(odd, pltpu.roll(wide_rows, 1, 0), -pltpu.roll(wide_rows, count - 1, 0))
    plain[...] = jnp.zeros_like(plain)
    plain[0, :, 0:channels] = stacked
    plain[1, :, 0:channels] = turned_rows.astype(jnp.bfloat16)
    source = iota((BLOCK, BLOCK), 0)
    spread = (
        2 * lax.rem(source, LANES) + source // LANES == iota((BLOCK, BLOCK), 1)
    ).astype(jnp.bfloat16)
    for t in range(WEIGHT_TILES):
        cols = slice(t * LANES, (t + 1) * LANES)
        pair = jnp.concatenate([plain[0, :, cols], plain[1, :, cols]], 1)
        block_rows[:, t * BLOCK : (t + 1) * BLOCK] = jnp.dot(
            pair, spread, preferred_element_type=jnp.float32
        ).astype(jnp.bfloat16)
    samples = held.reshape(GROUPS, 2 * channels, LANES)

    def form(i, carry):
        for h in range(SPAN):
            fetch(SPAN * i + h).wait()
        product = jnp.dot(
            block_rows[:, 0 : 2 * channels],
            jnp.concatenate([samples[SPAN * i + h] for h in range(SPAN)], 1),
            preferred_element_type=jnp.float32,
        )
        for h in range(SPAN):
            place = SPAN * i + h
            sums[pl.ds(place, count, stride=GROUPS), :] = product[:, h * LANES : (h + 1) * LANES]
        top = jnp.max(jnp.abs(product).reshape(count // 8, 8, SPAN * LANES), axis=0)
        return jnp.maximum(carry, top)

    nothing = jnp.zeros((8, SPAN * LANES), jnp.float32)
    blocks = GROUPS // SPAN

    def level_of(top):
        most = jnp.maximum(jnp.max(top, axis=(0, 1), keepdims=True), 1e-30)
        return jnp.broadcast_to(jnp.ceil(jnp.log2(most)), (16, LANES))

    def rows_of(owner, step):
        return pl.multiple_of((owner * BEAMS + STARTS[step]) * ROWS, ROWS)

    def packed(value, power):
        steps = value.reshape(-1, 16, LANES) * jnp.exp2(BITS - power)[None]
        return jnp.round(steps).astype(jnp.int32).astype(jnp.int16).reshape(-1, LANES)

    def unpacked(ref, count):
        power = ref[count : count + 16, :].astype(jnp.int32).astype(jnp.float32)
        steps = ref[0:count, :].astype(jnp.int32).astype(jnp.float32)
        value = steps.reshape(-1, 16, LANES) * jnp.exp2(power - BITS)[None]
        return value.reshape(count, LANES), power

    def ways(way):
        return 1 if way == 0 else 3

    def send_far(step, way):
        half = SIZES[step] * GROUPS
        rows = pl.ds(STARTS[step] * GROUPS + 16 * step, half + 16)
        return pltpu.make_async_remote_copy(
            src_ref=far_out.at[way, rows],
            dst_ref=early.at[way, rows],
            send_sem=a_send.at[step, way],
            recv_sem=a_recv.at[step, way],
            device_id=sub_to(ways(way)),
            device_id_type=MESH,
        )

    def near_rows(step):
        return pl.ds(STARTS[step] * ROWS + 16 * step, SIZES[step] * ROWS + 16)

    def send_near(step, way):
        rows = near_rows(step)
        return pltpu.make_async_remote_copy(
            src_ref=near_out.at[way, rows],
            dst_ref=late.at[way, rows],
            send_sem=b_send.at[step, way],
            recv_sem=b_recv.at[step, way],
            device_id=sub_to(ways(way)),
            device_id_type=MESH,
        )

    def launch(step):
        half = SIZES[step] * GROUPS
        place = STARTS[step] * GROUPS + 16 * step
        for way in range(2):
            start = rows_of(lax.rem(y + 2, SUBS), step) + way * half
            far_out[way, place : place + half, :] = packed(sums[pl.ds(start, half), :], level)
            far_out[way, place + half : place + half + 16, :] = (
                level.astype(jnp.int32).astype(jnp.int16)
            )
            send_far(step, way).start()

    def send_edge(step, way):
        lines = pl.ds(2 * STARTS[step], 2 * SIZES[step])
        return pltpu.make_async_remote_copy(
            src_ref=beams.at[2 * core, lines],
            dst_ref=beams.at[1 if way == 0 else 2 - 2 * core, lines],
            send_sem=h_send.at[step, way],
            recv_sem=h_recv.at[step, way],
            device_id=(y, d + 1 - 2 * core) if way == 0 else ring(4 * core - 2),
            device_id_type=MESH,
        )

    row = iota((256, NCODES), 0)
    code_of = lax.rem(
        2 * lax.rem(4 * lax.rem(row, GROUPS) + row // 64, 16) + based // 16, NCODES
    )
    code_hot = (code_of == iota((256, NCODES), 1)).astype(jnp.bfloat16)
    lane16 = iota((NBAUD, LANES), 1)
    baud_hot = jnp.where(
        (lax.rem(4 * based + lane16 // BAUD_LEN, NBAUD) == iota((NBAUD, LANES), 0)) & (lane16 < 96),
        1.0,
        0.0,
    ).astype(jnp.bfloat16)
    table = (2 * code_signs[...] - 1).astype(jnp.float32).astype(jnp.bfloat16)
    by_code = lax.dot_general(
        code_hot, table, (((1,), (1,)), ((), ())), preferred_element_type=jnp.float32
    ).astype(jnp.bfloat16)
    signs[...] = jnp.dot(by_code, baud_hot, preferred_element_type=jnp.float32).astype(jnp.bfloat16)

    def relay(step):
        half = SIZES[step] * GROUPS
        place = STARTS[step] * GROUPS + 16 * step
        spot = STARTS[step] * ROWS + 16 * step
        for way in range(2):
            send_far(step, way).wait_recv()
            start = rows_of(lax.rem(y + ways(way), SUBS), step)
            passed, power = unpacked(early.at[way, pl.ds(place, half + 16)], half)
            both = jnp.maximum(power, level) + 1
            mine, rest = way * half, (1 - way) * half
            near_out[way, spot + mine : spot + mine + half, :] = packed(
                sums[pl.ds(start + mine, half), :] + passed, both
            )
            near_out[way, spot + rest : spot + rest + half, :] = packed(
                sums[pl.ds(start + rest, half), :], both
            )
            near_out[way, spot + 2 * half : spot + 2 * half + 16, :] = (
                both.astype(jnp.int32).astype(jnp.int16)
            )
            send_near(step, way).start()

    def settle(step):
        part = SIZES[step] * ROWS
        total = sums[pl.ds(rows_of(y, step), part), :]
        for way in range(2):
            send_near(step, way).wait_recv()
            total += unpacked(late.at[way, near_rows(step)], part)[0]
        beams[2 * core, 2 * STARTS[step] : 2 * (STARTS[step] + SIZES[step])] = total.astype(
            jnp.bfloat16
        ).reshape(2 * SIZES[step], GROUPS, LANES)

    def share(step):
        for way in range(2):
            send_edge(step, way).start()

    def passed_end(slot, step):
        span = SIZES[step] * ROWS
        lines = slice(2 * STARTS[step], 2 * (STARTS[step] + SIZES[step]))
        turned = pltpu.roll(beams[slot, lines].reshape(span, LANES).astype(jnp.float32), 96, 1)
        above = pltpu.roll(turned, span - 1, 0)
        last = lax.rem(iota((span, LANES), 0), GROUPS) == GROUPS - 1
        new = jnp.where(iota((span, LANES), 1) < 96, turned, jnp.where(last, 0.0, above))
        beams[slot, lines] = new.astype(jnp.bfloat16).reshape(2 * SIZES[step], GROUPS, LANES)

    def correlate(step):
        for way in range(2):
            send_edge(step, way).wait()

        @pl.when(d == 1)
        def _():
            passed_end(1, step)

        @pl.when((d == 1) | (d == TMS - 2))
        def _():
            passed_end(2, step)

        size = SIZES[step]
        span = size * ROWS
        lane = iota((span, LANES), 1)
        offset = iota((span, LANES), 0)
        lines = slice(2 * STARTS[step], 2 * (STARTS[step] + size))
        three = [beams[slot, lines].reshape(span, LANES) for slot in range(3)]
        for c in range(4):
            here, n1, n2 = [
                pltpu.roll(v, shift, 1) if shift else v
                for v, shift in ((v, (128 + 32 * (j - c)) % 128) for j, v in enumerate(three))
            ]
            mixed = jnp.where(lane < 32, here, jnp.where(lane < 64, n1, n2))
            mixed = mixed.reshape(size, ROWS, LANES) * signs[c * ROWS : (c + 1) * ROWS, :][None]
            coded[0:size, :, c] = mixed.reshape(size, 2, GROUPS, LANES)
        grams = []
        low = iota((256, LANES), 1) < 32
        for k in range(size):
            later = coded[k].reshape(256, LANES)
            turned = jnp.concatenate([-later[128:], later[:128]], 0)
            base = jnp.where(low, later, pltpu.roll(turned, 32, 1))
            gram = lax.dot_general(
                base, later, (((0,), (0,)), ((), ())), preferred_element_type=jnp.float32
            )
            real = jnp.concatenate(
                [pltpu.roll(gram[r : r + 8], 127 - r, 1) for r in (0, 8, 16, 24)], 0
            )
            imag = jnp.concatenate(
                [pltpu.roll(gram[r + 32 : r + 40], (191 - r) % 128, 1) for r in (0, 8, 16, 24)], 0
            )
            grams += [real, imag]
        gram = jnp.concatenate(grams, 0)
        for bit in (1, 2, 4):
            gram = jnp.where((offset & bit) > 0, pltpu.roll(gram, LANES - bit, 1), gram)
        gram = gram.reshape(size, 2, 32, LANES)
        skewed[0 : size * 32] = jnp.where(
            iota((size, 32, LANES), 2) < LAGS, gram[:, 0], gram[:, 1]
        ).reshape(size * 32, LANES)
        even = skewed[pl.ds(0, size * 16, stride=2), :]
        pairs = even + skewed[pl.ds(1, size * 16, stride=2), :]
        for k in range(size):
            place = (STARTS[step] + k) * LANES
            row_sec[z, :, place : place + LANES] = pairs[16 * k : 16 * k + 16].astype(
                jnp.bfloat16
            )

    def cols_of(step):
        return pl.ds(STARTS[step] * LANES, SIZES[step] * LANES)

    def send_z(step, i):
        return pltpu.make_async_remote_copy(
            src_ref=row_sec.at[z, :, cols_of(step)],
            dst_ref=row_sec.at[z, :, cols_of(step)],
            send_sem=z_send.at[step, i - 1],
            recv_sem=z_recv.at[step, i - 1],
            device_id=z_to(i),
            device_id_type=MESH,
        )

    def send_gates(step, i):
        return pltpu.make_async_remote_copy(
            src_ref=picked.at[lax.rem(d + i, 8), :, cols_of(step)],
            dst_ref=gate_part.at[i - 1, :, cols_of(step)],
            send_sem=g_send.at[step, i - 1],
            recv_sem=g_recv.at[step, i - 1],
            device_id=row_to(i),
            device_id_type=MESH,
        )

    fetch_gates.wait()
    gate_row = z * 32 + iota((32, NSEC), 0)
    named = (raw_gates[...] == gate_row).astype(jnp.bfloat16)
    col = iota((NSEC, 64), 1)
    origin = lax.rem(col // 16 * 8 + lax.rem(d, 8) + TMS - 2 * core, 16)
    section = 16 * origin + lax.rem(col, 16)
    chosen = (iota((NSEC, 64), 0) == section).astype(jnp.bfloat16)
    scale = 1.0 / math.sqrt(TMS * T_DEV / GATES)
    gate_hot = jnp.dot(named, chosen, preferred_element_type=jnp.float32).astype(jnp.bfloat16)

    def route(step):
        for i in (1, 2, 3):
            send_z(step, i).wait_recv()
        gathered = row_sec[:, :, cols_of(step)].reshape(64, SIZES[step] * LANES)
        gates = jnp.dot(gate_hot, gathered, preferred_element_type=jnp.float32) * scale
        for k in range(8):
            picked[k, :, cols_of(step)] = gates[4 * k : 4 * k + 4]
        for i in range(1, 8):
            send_gates(step, i).start()

    def finish(step):
        total = picked[lax.rem(d, 8), :, cols_of(step)]
        for i in range(1, 8):
            send_gates(step, i).wait_recv()
            total += gate_part[i - 1, :, cols_of(step)]
        out[:, cols_of(step)] = total

    level = level_of(lax.fori_loop(0, blocks, form, nothing))
    pl.semaphore_wait(barrier, len(met))
    for s in range(AHEAD):
        launch(s)
    for s in range(STEPS + LAG_ROUTE):
        if s + AHEAD < STEPS:
            launch(s + AHEAD)
        if s < STEPS:
            relay(s)
        if 1 <= s <= STEPS:
            settle(s - 1)
            share(s - 1)
        if 0 <= s - LAG_PAIR < STEPS:
            correlate(s - LAG_PAIR)
            for i in (1, 2, 3):
                send_z(s - LAG_PAIR, i).start()
        if 0 <= s - LAG_ROUTE:
            route(s - LAG_ROUTE)
    for step in range(STEPS):
        finish(step)

    for step in range(STEPS):
        for way in range(2):
            send_far(step, way).wait_send()
            send_near(step, way).wait_send()
        for i in (1, 2, 3):
            send_z(step, i).wait_send()
        for i in range(1, 8):
            send_gates(step, i).wait_send()


def body(streams, beam_weights, code_signs, gate_map):
    dma = pltpu.SemaphoreType.DMA
    channels = streams.shape[1]
    tiles = streams.reshape(2, channels, GROUPS, LANES).transpose(1, 2, 0, 3)
    paired = beam_weights.transpose(1, 0, 2)
    f32, bf16, i16 = jnp.float32, jnp.bfloat16, jnp.int16
    vmem = pl.BlockSpec(memory_space=pltpu.VMEM)
    hbm = pl.BlockSpec(memory_space=pltpu.HBM)
    summed = pl.pallas_call(
        kernel,
        out_shape=jax.ShapeDtypeStruct((4, WIDE), f32),
        in_specs=[hbm, hbm, vmem, hbm],
        out_specs=vmem,
        scratch_shapes=[
            pltpu.VMEM((GROUPS, channels, 2, LANES), bf16),
            pltpu.VMEM((100, 2, channels), bf16),
            pltpu.VMEM((1, NSEC), jnp.int32),
            pltpu.VMEM((2, 200, WEIGHT_TILES * LANES), bf16),
            pltpu.VMEM((200, WEIGHT_TILES * BLOCK), bf16),
            pltpu.VMEM((100 * ROWS, LANES), f32),
            pltpu.VMEM((2, BEAMS * GROUPS + 16 * STEPS, LANES), i16),
            pltpu.VMEM((2, BEAMS * ROWS + 16 * STEPS, LANES), i16),
            pltpu.VMEM((3, 2 * BEAMS, GROUPS, LANES), bf16),
            pltpu.VMEM((256, LANES), bf16),
            pltpu.VMEM((MOST, 2, 4, GROUPS, LANES), bf16),
            pltpu.VMEM((MOST * 32, LANES), f32),
            pltpu.VMEM((4, 16, WIDE), bf16),
            pltpu.VMEM((8, 4, WIDE), f32),
            pltpu.VMEM((7, 4, WIDE), f32),
            pltpu.VMEM((2, BEAMS * GROUPS + 16 * STEPS, LANES), i16),
            pltpu.VMEM((2, BEAMS * ROWS + 16 * STEPS, LANES), i16),
            dma((GROUPS,)), dma((2,)),
            dma((STEPS, 2)), dma((STEPS, 2)), dma((STEPS, 2)), dma((STEPS, 2)),
            dma((STEPS, 2)), dma((STEPS, 2)),
            dma((STEPS, 3)), dma((STEPS, 3)), dma((STEPS, 7)), dma((STEPS, 7)),
        ],
        compiler_params=pltpu.CompilerParams(
            collective_id=0, has_side_effects=True, vmem_limit_bytes=58 * 2**20
        ),
    )(tiles, paired, code_signs.T, gate_map.reshape(1, NSEC))
    return summed.reshape(4, BEAMS, LANES)


def solution(mesh):
    placed = (P(None, "sub", "tm"), P(None, None, "sub"), P(), P())
    return jax.shard_map(
        body, mesh=mesh, in_specs=placed, out_specs=P("tm", "sub", None), check_vma=False
    )
```

```python
import functools
import math

import jax
import jax.numpy as jnp
from jax import lax
from jax.experimental import pallas as pl
from jax.experimental.pallas import tpu as pltpu
from jax.sharding import PartitionSpec as P

PKT = 32
IPP_LEN = 512
LAGS = 64
NCODES = 32
NBAUD = 16
BAUD_LEN = 8
SEC_LEN = 2
GATES = 128
NSEC = 256
LANES = 128
SUBS = 4
TMS = 32
BEAMS = 25
T_DEV = 4096
GROUPS = T_DEV // LANES
ROWS = 2 * GROUPS
SPAN = 4
WEIGHT_TILES = 5
SIZES = (6, 6, 5, 4, 4)
STARTS = (0, 6, 12, 17, 21)
STEPS = len(SIZES)
MOST = max(SIZES)
BLOCK = 256
WIDE = BEAMS * LANES
BITS = 14.9
MESH = pl.DeviceIdType.MESH


def iota(shape, dim):
    return lax.broadcasted_iota(jnp.int32, shape, dim)


def kernel(
    streams, weights, code_signs, gate_map, out,
    held, raw_weights, raw_gates, plain, block_rows, sums, early, late, beams, signs,
    coded, skewed, row_sec, picked, gate_part, far_out, near_out,
    in_sem, w_sem, a_send, a_recv, b_send, b_recv, h_send, h_recv, z_send, z_recv, g_send, g_recv,
):
    y = lax.axis_index("sub")
    d = lax.axis_index("tm")
    z = d // 8
    core = lax.rem(d, 2)
    based = lax.rem(d + TMS - 2 * core, TMS)

    def ring(step):
        return (y, lax.rem(d + step + TMS, TMS))

    def sub_to(step):
        return (lax.rem(y + step, SUBS), d)

    def z_to(step):
        return (y, lax.rem(z + step, 4) * 8 + lax.rem(d, 8))

    def row_to(step):
        return (y, z * 8 + lax.rem(d + step, 8))

    def fetch(i):
        return pltpu.make_async_copy(streams.at[:, i], held.at[i], in_sem.at[i])

    fetch_weights = pltpu.make_async_copy(weights, raw_weights, w_sem.at[0])
    fetch_gates = pltpu.make_async_copy(gate_map, raw_gates, w_sem.at[1])
    fetch_weights.start()
    for i in range(GROUPS):
        fetch(i).start()
    fetch_gates.start()

    barrier = pltpu.get_barrier_semaphore()
    met = [sub_to(1), sub_to(3), ring(-2), ring(2)]
    met += [z_to(i) for i in (1, 2, 3)] + [row_to(i) for i in range(1, 8)]
    for device in met:
        pl.semaphore_signal(barrier, inc=1, device_id=device, device_id_type=MESH)

    channels = weights.shape[2]
    fetch_weights.wait()
    stacked = raw_weights[...].reshape(2 * weights.shape[0], channels)
    wide_rows = stacked.astype(jnp.float32)
    count = wide_rows.shape[0]
    odd = lax.rem(iota(wide_rows.shape, 0), 2) == 1
    turned_rows = jnp.where(odd, pltpu.roll(wide_rows, 1, 0), -pltpu.roll(wide_rows, count - 1, 0))
    plain[...] = jnp.zeros_like(plain)
    plain[0, :, 0:channels] = stacked
    plain[1, :, 0:channels] = turned_rows.astype(jnp.bfloat16)
    source = iota((BLOCK, BLOCK), 0)
    spread = (
        2 * lax.rem(source, LANES) + source // LANES == iota((BLOCK, BLOCK), 1)
    ).astype(jnp.bfloat16)
    for t in range(WEIGHT_TILES):
        cols = slice(t * LANES, (t + 1) * LANES)
        pair = jnp.concatenate([plain[0, :, cols], plain[1, :, cols]], 1)
        block_rows[:, t * BLOCK : (t + 1) * BLOCK] = jnp.dot(
            pair, spread, preferred_element_type=jnp.float32
        ).astype(jnp.bfloat16)
    samples = held.reshape(GROUPS, 2 * channels, LANES)

    def form(i, carry):
        for h in range(SPAN):
            fetch(SPAN * i + h).wait()
        product = jnp.dot(
            block_rows[:, 0 : 2 * channels],
            jnp.concatenate([samples[SPAN * i + h] for h in range(SPAN)], 1),
            preferred_element_type=jnp.float32,
        )
        for h in range(SPAN):
            place = SPAN * i + h
            sums[pl.ds(place, count, stride=GROUPS), :] = product[:, h * LANES : (h + 1) * LANES]
        top = jnp.max(jnp.abs(product).reshape(count // 8, 8, SPAN * LANES), axis=0)
        return jnp.maximum(carry, top)

    nothing = jnp.zeros((8, SPAN * LANES), jnp.float32)
    blocks = GROUPS // SPAN

    def level_of(top):
        most = jnp.maximum(jnp.max(top, axis=(0, 1), keepdims=True), 1e-30)
        return jnp.broadcast_to(jnp.ceil(jnp.log2(most)), (16, LANES))

    def rows_of(owner, step):
        return pl.multiple_of((owner * BEAMS + STARTS[step]) * ROWS, ROWS)

    def packed(value, power):
        steps = value.reshape(-1, 16, LANES) * jnp.exp2(BITS - power)[None]
        return jnp.round(steps).astype(jnp.int32).astype(jnp.int16).reshape(-1, LANES)

    def unpacked(ref, count):
        power = ref[count : count + 16, :].astype(jnp.int32).astype(jnp.float32)
        steps = ref[0:count, :].astype(jnp.int32).astype(jnp.float32)
        value = steps.reshape(-1, 16, LANES) * jnp.exp2(power - BITS)[None]
        return value.reshape(count, LANES), power

    def ways(way):
        return 1 if way == 0 else 3

    def send_far(step, way):
        half = SIZES[step] * GROUPS
        rows = pl.ds(STARTS[step] * GROUPS + 16 * step, half + 16)
        return pltpu.make_async_remote_copy(
            src_ref=far_out.at[way, rows],
            dst_ref=early.at[way, rows],
            send_sem=a_send.at[step, way],
            recv_sem=a_recv.at[step, way],
            device_id=sub_to(ways(way)),
            device_id_type=MESH,
        )

    def near_rows(step):
        return pl.ds(STARTS[step] * ROWS + 16 * step, SIZES[step] * ROWS + 16)

    def send_near(step, way):
        rows = near_rows(step)
        return pltpu.make_async_remote_copy(
            src_ref=near_out.at[way, rows],
            dst_ref=late.at[way, rows],
            send_sem=b_send.at[step, way],
            recv_sem=b_recv.at[step, way],
            device_id=sub_to(ways(way)),
            device_id_type=MESH,
        )

    def launch(step):
        half = SIZES[step] * GROUPS
        place = STARTS[step] * GROUPS + 16 * step
        for way in range(2):
            start = rows_of(lax.rem(y + 2, SUBS), step) + way * half
            far_out[way, place : place + half, :] = packed(sums[pl.ds(start, half), :], level)
            far_out[way, place + half : place + half + 16, :] = (
                level.astype(jnp.int32).astype(jnp.int16)
            )
            send_far(step, way).start()

    def send_edge(step, way):
        lines = pl.ds(2 * STARTS[step], 2 * SIZES[step])
        return pltpu.make_async_remote_copy(
            src_ref=beams.at[2 * core, lines],
            dst_ref=beams.at[1 if way == 0 else 2 - 2 * core, lines],
            send_sem=h_send.at[step, way],
            recv_sem=h_recv.at[step, way],
            device_id=(y, d + 1 - 2 * core) if way == 0 else ring(4 * core - 2),
            device_id_type=MESH,
        )

    row = iota((256, NCODES), 0)
    code_of = lax.rem(
        2 * lax.rem(4 * lax.rem(row, GROUPS) + row // 64, 16) + based // 16, NCODES
    )
    code_hot = (code_of == iota((256, NCODES), 1)).astype(jnp.bfloat16)
    lane16 = iota((NBAUD, LANES), 1)
    baud_hot = jnp.where(
        (lax.rem(4 * based + lane16 // BAUD_LEN, NBAUD) == iota((NBAUD, LANES), 0)) & (lane16 < 96),
        1.0,
        0.0,
    ).astype(jnp.bfloat16)
    table = (2 * code_signs[...] - 1).astype(jnp.float32).astype(jnp.bfloat16)
    by_code = lax.dot_general(
        code_hot, table, (((1,), (1,)), ((), ())), preferred_element_type=jnp.float32
    ).astype(jnp.bfloat16)
    signs[...] = jnp.dot(by_code, baud_hot, preferred_element_type=jnp.float32).astype(jnp.bfloat16)

    def relay(step):
        half = SIZES[step] * GROUPS
        place = STARTS[step] * GROUPS + 16 * step
        spot = STARTS[step] * ROWS + 16 * step
        for way in range(2):
            send_far(step, way).wait_recv()
            start = rows_of(lax.rem(y + ways(way), SUBS), step)
            passed, power = unpacked(early.at[way, pl.ds(place, half + 16)], half)
            both = jnp.maximum(power, level) + 1
            mine, rest = way * half, (1 - way) * half
            near_out[way, spot + mine : spot + mine + half, :] = packed(
                sums[pl.ds(start + mine, half), :] + passed, both
            )
            near_out[way, spot + rest : spot + rest + half, :] = packed(
                sums[pl.ds(start + rest, half), :], both
            )
            near_out[way, spot + 2 * half : spot + 2 * half + 16, :] = (
                both.astype(jnp.int32).astype(jnp.int16)
            )
            send_near(step, way).start()

    def settle(step):
        part = SIZES[step] * ROWS
        total = sums[pl.ds(rows_of(y, step), part), :]
        for way in range(2):
            send_near(step, way).wait_recv()
            total += unpacked(late.at[way, near_rows(step)], part)[0]
        beams[2 * core, 2 * STARTS[step] : 2 * (STARTS[step] + SIZES[step])] = total.astype(
            jnp.bfloat16
        ).reshape(2 * SIZES[step], GROUPS, LANES)

    def share(step):
        for way in range(2):
            send_edge(step, way).start()

    def passed_end(slot, step):
        span = SIZES[step] * ROWS
        lines = slice(2 * STARTS[step], 2 * (STARTS[step] + SIZES[step]))
        turned = pltpu.roll(beams[slot, lines].reshape(span, LANES).astype(jnp.float32), 96, 1)
        above = pltpu.roll(turned, span - 1, 0)
        last = lax.rem(iota((span, LANES), 0), GROUPS) == GROUPS - 1
        new = jnp.where(iota((span, LANES), 1) < 96, turned, jnp.where(last, 0.0, above))
        beams[slot, lines] = new.astype(jnp.bfloat16).reshape(2 * SIZES[step], GROUPS, LANES)

    def correlate(step):
        for way in range(2):
            send_edge(step, way).wait()

        @pl.when(d == 1)
        def _():
            passed_end(1, step)

        @pl.when((d == 1) | (d == TMS - 2))
        def _():
            passed_end(2, step)

        size = SIZES[step]
        span = size * ROWS
        lane = iota((span, LANES), 1)
        offset = iota((span, LANES), 0)
        lines = slice(2 * STARTS[step], 2 * (STARTS[step] + size))
        three = [beams[slot, lines].reshape(span, LANES) for slot in range(3)]
        for c in range(4):
            here, n1, n2 = [
                pltpu.roll(v, shift, 1) if shift else v
                for v, shift in ((v, (128 + 32 * (j - c)) % 128) for j, v in enumerate(three))
            ]
            mixed = jnp.where(lane < 32, here, jnp.where(lane < 64, n1, n2))
            mixed = mixed.reshape(size, ROWS, LANES) * signs[c * ROWS : (c + 1) * ROWS, :][None]
            coded[0:size, :, c] = mixed.reshape(size, 2, GROUPS, LANES)
        grams = []
        low = iota((256, LANES), 1) < 32
        for k in range(size):
            later = coded[k].reshape(256, LANES)
            turned = jnp.concatenate([-later[128:], later[:128]], 0)
            base = jnp.where(low, later, pltpu.roll(turned, 32, 1))
            gram = lax.dot_general(
                base, later, (((0,), (0,)), ((), ())), preferred_element_type=jnp.float32
            )
            real = jnp.concatenate(
                [pltpu.roll(gram[r : r + 8], 127 - r, 1) for r in (0, 8, 16, 24)], 0
            )
            imag = jnp.concatenate(
                [pltpu.roll(gram[r + 32 : r + 40], (191 - r) % 128, 1) for r in (0, 8, 16, 24)], 0
            )
            grams += [real, imag]
        gram = jnp.concatenate(grams, 0)
        for bit in (1, 2, 4):
            gram = jnp.where((offset & bit) > 0, pltpu.roll(gram, LANES - bit, 1), gram)
        gram = gram.reshape(size, 2, 32, LANES)
        skewed[0 : size * 32] = jnp.where(
            iota((size, 32, LANES), 2) < LAGS, gram[:, 0], gram[:, 1]
        ).reshape(size * 32, LANES)
        even = skewed[pl.ds(0, size * 16, stride=2), :]
        pairs = even + skewed[pl.ds(1, size * 16, stride=2), :]
        for k in range(size):
            place = (STARTS[step] + k) * LANES
            row_sec[z, :, place : place + LANES] = pairs[16 * k : 16 * k + 16].astype(
                jnp.bfloat16
            )

    def cols_of(step):
        return pl.ds(STARTS[step] * LANES, SIZES[step] * LANES)

    def send_z(step, i):
        return pltpu.make_async_remote_copy(
            src_ref=row_sec.at[z, :, cols_of(step)],
            dst_ref=row_sec.at[z, :, cols_of(step)],
            send_sem=z_send.at[step, i - 1],
            recv_sem=z_recv.at[step, i - 1],
            device_id=z_to(i),
            device_id_type=MESH,
        )

    def send_gates(step, i):
        return pltpu.make_async_remote_copy(
            src_ref=picked.at[lax.rem(d + i, 8), :, cols_of(step)],
            dst_ref=gate_part.at[i - 1, :, cols_of(step)],
            send_sem=g_send.at[step, i - 1],
            recv_sem=g_recv.at[step, i - 1],
            device_id=row_to(i),
            device_id_type=MESH,
        )

    fetch_gates.wait()
    gate_row = z * 32 + iota((32, NSEC), 0)
    named = (raw_gates[...] == gate_row).astype(jnp.bfloat16)
    col = iota((NSEC, 64), 1)
    origin = lax.rem(col // 16 * 8 + lax.rem(d, 8) + TMS - 2 * core, 16)
    section = 16 * origin + lax.rem(col, 16)
    chosen = (iota((NSEC, 64), 0) == section).astype(jnp.bfloat16)
    scale = 1.0 / math.sqrt(TMS * T_DEV / GATES)
    gate_hot = jnp.dot(named, chosen, preferred_element_type=jnp.float32).astype(jnp.bfloat16)

    def route(step):
        for i in (1, 2, 3):
            send_z(step, i).wait_recv()
        gathered = row_sec[:, :, cols_of(step)].reshape(64, SIZES[step] * LANES)
        gates = jnp.dot(gate_hot, gathered, preferred_element_type=jnp.float32) * scale
        for k in range(8):
            picked[k, :, cols_of(step)] = gates[4 * k : 4 * k + 4]
        for i in range(1, 8):
            send_gates(step, i).start()

    def finish(step):
        total = picked[lax.rem(d, 8), :, cols_of(step)]
        for i in range(1, 8):
            send_gates(step, i).wait_recv()
            total += gate_part[i - 1, :, cols_of(step)]
        out[:, cols_of(step)] = total

    level = level_of(lax.fori_loop(0, blocks, form, nothing))
    pl.semaphore_wait(barrier, len(met))
    for step in range(STEPS):
        launch(step)
    for step in range(STEPS):
        relay(step)
    for step in range(STEPS):
        settle(step)
        share(step)
    for step in range(STEPS):
        correlate(step)
        for i in (1, 2, 3):
            send_z(step, i).start()
    for step in range(STEPS):
        route(step)
    for step in range(STEPS):
        finish(step)

    for step in range(STEPS):
        for way in range(2):
            send_far(step, way).wait_send()
            send_near(step, way).wait_send()
        for i in (1, 2, 3):
            send_z(step, i).wait_send()
        for i in range(1, 8):
            send_gates(step, i).wait_send()


def body(streams, beam_weights, code_signs, gate_map):
    dma = pltpu.SemaphoreType.DMA
    channels = streams.shape[1]
    tiles = streams.reshape(2, channels, GROUPS, LANES).transpose(1, 2, 0, 3)
    paired = beam_weights.transpose(1, 0, 2)
    f32, bf16, i16 = jnp.float32, jnp.bfloat16, jnp.int16
    vmem = pl.BlockSpec(memory_space=pltpu.VMEM)
    hbm = pl.BlockSpec(memory_space=pltpu.HBM)
    summed = pl.pallas_call(
        kernel,
        out_shape=jax.ShapeDtypeStruct((4, WIDE), f32),
        in_specs=[hbm, hbm, vmem, hbm],
        out_specs=vmem,
        scratch_shapes=[
            pltpu.VMEM((GROUPS, channels, 2, LANES), bf16),
            pltpu.VMEM((100, 2, channels), bf16),
            pltpu.VMEM((1, NSEC), jnp.int32),
            pltpu.VMEM((2, 200, WEIGHT_TILES * LANES), bf16),
            pltpu.VMEM((200, WEIGHT_TILES * BLOCK), bf16),
            pltpu.VMEM((100 * ROWS, LANES), f32),
            pltpu.VMEM((2, BEAMS * GROUPS + 16 * STEPS, LANES), i16),
            pltpu.VMEM((2, BEAMS * ROWS + 16 * STEPS, LANES), i16),
            pltpu.VMEM((3, 2 * BEAMS, GROUPS, LANES), bf16),
            pltpu.VMEM((256, LANES), bf16),
            pltpu.VMEM((MOST, 2, 4, GROUPS, LANES), bf16),
            pltpu.VMEM((MOST * 32, LANES), f32),
            pltpu.VMEM((4, 16, WIDE), bf16),
            pltpu.VMEM((8, 4, WIDE), f32),
            pltpu.VMEM((7, 4, WIDE), f32),
            pltpu.VMEM((2, BEAMS * GROUPS + 16 * STEPS, LANES), i16),
            pltpu.VMEM((2, BEAMS * ROWS + 16 * STEPS, LANES), i16),
            dma((GROUPS,)), dma((2,)),
            dma((STEPS, 2)), dma((STEPS, 2)), dma((STEPS, 2)), dma((STEPS, 2)),
            dma((STEPS, 2)), dma((STEPS, 2)),
            dma((STEPS, 3)), dma((STEPS, 3)), dma((STEPS, 7)), dma((STEPS, 7)),
        ],
        compiler_params=pltpu.CompilerParams(
            collective_id=0, has_side_effects=True, vmem_limit_bytes=48 * 2**20
        ),
    )(tiles, paired, code_signs.T, gate_map.reshape(1, NSEC))
    return summed.reshape(4, BEAMS, LANES)


def solution(mesh):
    placed = (P(None, "sub", "tm"), P(None, None, "sub"), P(), P())
    return jax.shard_map(
        body, mesh=mesh, in_specs=placed, out_specs=P("tm", "sub", None), check_vma=False
    )
```

```python
import functools
import math

import jax
import jax.numpy as jnp
from jax import lax
from jax.experimental import pallas as pl
from jax.experimental.pallas import tpu as pltpu
from jax.sharding import PartitionSpec as P

PKT = 32
IPP_LEN = 512
LAGS = 64
NCODES = 32
NBAUD = 16
BAUD_LEN = 8
SEC_LEN = 2
GATES = 128
NSEC = 256
LANES = 128
SUBS = 4
TMS = 32
BEAMS = 25
T_DEV = 4096
GROUPS = T_DEV // LANES
ROWS = 2 * GROUPS
SPAN = 4
WEIGHT_TILES = 5
SIZES = (6, 6, 5, 4, 4)
STARTS = (0, 6, 12, 17, 21)
STEPS = len(SIZES)
MOST = max(SIZES)
BLOCK = 256
WIDE = BEAMS * LANES
BITS = 14.9
MESH = pl.DeviceIdType.MESH


def iota(shape, dim):
    return lax.broadcasted_iota(jnp.int32, shape, dim)


def kernel(
    streams, weights, code_signs, gate_map, out,
    held, raw_weights, raw_gates, plain, block_rows, sums, early, late, beams, signs,
    coded, skewed, row_sec, picked, gate_part, far_out, near_out,
    in_sem, w_sem, a_send, a_recv, b_send, b_recv, h_send, h_recv, z_send, z_recv, g_send, g_recv,
):
    y = lax.axis_index("sub")
    d = lax.axis_index("tm")
    z = d // 8
    core = lax.rem(d, 2)
    based = lax.rem(d + TMS - 2 * core, TMS)

    def ring(step):
        return (y, lax.rem(d + step + TMS, TMS))

    def sub_to(step):
        return (lax.rem(y + step, SUBS), d)

    def z_to(step):
        return (y, lax.rem(z + step, 4) * 8 + lax.rem(d, 8))

    def row_to(step):
        return (y, z * 8 + lax.rem(d + step, 8))

    def fetch(i):
        return pltpu.make_async_copy(streams.at[:, i], held.at[i], in_sem.at[i])

    fetch_weights = pltpu.make_async_copy(weights, raw_weights, w_sem.at[0])
    fetch_gates = pltpu.make_async_copy(gate_map, raw_gates, w_sem.at[1])
    fetch_weights.start()
    for i in range(GROUPS):
        fetch(i).start()
    fetch_gates.start()

    barrier = pltpu.get_barrier_semaphore()
    met = [sub_to(1), sub_to(3), ring(-2), ring(2)]
    met += [z_to(i) for i in (1, 2, 3)] + [row_to(i) for i in range(1, 8)]
    for device in met:
        pl.semaphore_signal(barrier, inc=1, device_id=device, device_id_type=MESH)

    channels = weights.shape[2]
    fetch_weights.wait()
    stacked = raw_weights[...].reshape(2 * weights.shape[0], channels)
    wide_rows = stacked.astype(jnp.float32)
    count = wide_rows.shape[0]
    odd = lax.rem(iota(wide_rows.shape, 0), 2) == 1
    turned_rows = jnp.where(odd, pltpu.roll(wide_rows, 1, 0), -pltpu.roll(wide_rows, count - 1, 0))
    plain[...] = jnp.zeros_like(plain)
    plain[0, :, 0:channels] = stacked
    plain[1, :, 0:channels] = turned_rows.astype(jnp.bfloat16)
    source = iota((BLOCK, BLOCK), 0)
    spread = (
        2 * lax.rem(source, LANES) + source // LANES == iota((BLOCK, BLOCK), 1)
    ).astype(jnp.bfloat16)
    for t in range(WEIGHT_TILES):
        cols = slice(t * LANES, (t + 1) * LANES)
        pair = jnp.concatenate([plain[0, :, cols], plain[1, :, cols]], 1)
        block_rows[:, t * BLOCK : (t + 1) * BLOCK] = jnp.dot(
            pair, spread, preferred_element_type=jnp.float32
        ).astype(jnp.bfloat16)
    samples = held.reshape(GROUPS, 2 * channels, LANES)

    def form(i, carry):
        for h in range(SPAN):
            fetch(SPAN * i + h).wait()
        product = jnp.dot(
            block_rows[:, 0 : 2 * channels],
            jnp.concatenate([samples[SPAN * i + h] for h in range(SPAN)], 1),
            preferred_element_type=jnp.float32,
        )
        for h in range(SPAN):
            place = SPAN * i + h
            sums[pl.ds(place, count, stride=GROUPS), :] = product[:, h * LANES : (h + 1) * LANES]
        top = jnp.max(jnp.abs(product).reshape(count // 8, 8, SPAN * LANES), axis=0)
        return jnp.maximum(carry, top)

    nothing = jnp.zeros((8, SPAN * LANES), jnp.float32)
    blocks = GROUPS // SPAN

    def level_of(top):
        most = jnp.maximum(jnp.max(top, axis=(0, 1), keepdims=True), 1e-30)
        return jnp.broadcast_to(jnp.ceil(jnp.log2(most)), (16, LANES))

    def rows_of(owner, step):
        return pl.multiple_of((owner * BEAMS + STARTS[step]) * ROWS, ROWS)

    def packed(value, power):
        steps = value.reshape(-1, 16, LANES) * jnp.exp2(BITS - power)[None]
        return jnp.round(steps).astype(jnp.int32).astype(jnp.int16).reshape(-1, LANES)

    def unpacked(ref, count):
        power = ref[count : count + 16, :].astype(jnp.int32).astype(jnp.float32)
        steps = ref[0:count, :].astype(jnp.int32).astype(jnp.float32)
        value = steps.reshape(-1, 16, LANES) * jnp.exp2(power - BITS)[None]
        return value.reshape(count, LANES), power

    def ways(way):
        return 1 if way == 0 else 3

    def send_far(step, way):
        half = SIZES[step] * GROUPS
        rows = pl.ds(STARTS[step] * GROUPS + 16 * step, half + 16)
        return pltpu.make_async_remote_copy(
            src_ref=far_out.at[way, rows],
            dst_ref=early.at[way, rows],
            send_sem=a_send.at[step, way],
            recv_sem=a_recv.at[step, way],
            device_id=sub_to(ways(way)),
            device_id_type=MESH,
        )

    def near_rows(step):
        return pl.ds(STARTS[step] * ROWS + 16 * step, SIZES[step] * ROWS + 16)

    def send_near(step, way):
        rows = near_rows(step)
        return pltpu.make_async_remote_copy(
            src_ref=near_out.at[way, rows],
            dst_ref=late.at[way, rows],
            send_sem=b_send.at[step, way],
            recv_sem=b_recv.at[step, way],
            device_id=sub_to(ways(way)),
            device_id_type=MESH,
        )

    def launch(step):
        half = SIZES[step] * GROUPS
        place = STARTS[step] * GROUPS + 16 * step
        for way in range(2):
            start = rows_of(lax.rem(y + 2, SUBS), step) + way * half
            far_out[way, place : place + half, :] = packed(sums[pl.ds(start, half), :], level)
            far_out[way, place + half : place + half + 16, :] = (
                level.astype(jnp.int32).astype(jnp.int16)
            )
            send_far(step, way).start()

    def send_edge(step, way):
        lines = pl.ds(2 * STARTS[step], 2 * SIZES[step])
        return pltpu.make_async_remote_copy(
            src_ref=beams.at[2 * core, lines],
            dst_ref=beams.at[1 if way == 0 else 2 - 2 * core, lines],
            send_sem=h_send.at[step, way],
            recv_sem=h_recv.at[step, way],
            device_id=(y, d + 1 - 2 * core) if way == 0 else ring(4 * core - 2),
            device_id_type=MESH,
        )

    row = iota((256, NCODES), 0)
    code_of = lax.rem(
        2 * lax.rem(4 * lax.rem(row, GROUPS) + row // 64, 16) + based // 16, NCODES
    )
    code_hot = (code_of == iota((256, NCODES), 1)).astype(jnp.bfloat16)
    lane16 = iota((NBAUD, LANES), 1)
    baud_hot = jnp.where(
        (lax.rem(4 * based + lane16 // BAUD_LEN, NBAUD) == iota((NBAUD, LANES), 0)) & (lane16 < 96),
        1.0,
        0.0,
    ).astype(jnp.bfloat16)
    table = (2 * code_signs[...] - 1).astype(jnp.float32).astype(jnp.bfloat16)
    by_code = lax.dot_general(
        code_hot, table, (((1,), (1,)), ((), ())), preferred_element_type=jnp.float32
    ).astype(jnp.bfloat16)
    signs[...] = jnp.dot(by_code, baud_hot, preferred_element_type=jnp.float32).astype(jnp.bfloat16)

    def relay(step):
        half = SIZES[step] * GROUPS
        place = STARTS[step] * GROUPS + 16 * step
        spot = STARTS[step] * ROWS + 16 * step
        for way in range(2):
            send_far(step, way).wait_recv()
            start = rows_of(lax.rem(y + ways(way), SUBS), step)
            passed, power = unpacked(early.at[way, pl.ds(place, half + 16)], half)
            both = jnp.maximum(power, level) + 1
            mine, rest = way * half, (1 - way) * half
            near_out[way, spot + mine : spot + mine + half, :] = packed(
                sums[pl.ds(start + mine, half), :] + passed, both
            )
            near_out[way, spot + rest : spot + rest + half, :] = packed(
                sums[pl.ds(start + rest, half), :], both
            )
            near_out[way, spot + 2 * half : spot + 2 * half + 16, :] = (
                both.astype(jnp.int32).astype(jnp.int16)
            )
            send_near(step, way).start()

    def settle(step):
        part = SIZES[step] * ROWS
        total = sums[pl.ds(rows_of(y, step), part), :]
        for way in range(2):
            send_near(step, way).wait_recv()
            total += unpacked(late.at[way, near_rows(step)], part)[0]
        beams[2 * core, 2 * STARTS[step] : 2 * (STARTS[step] + SIZES[step])] = total.astype(
            jnp.bfloat16
        ).reshape(2 * SIZES[step], GROUPS, LANES)

    def share(step):
        for way in range(2):
            send_edge(step, way).start()

    def passed_end(slot, step):
        span = SIZES[step] * ROWS
        lines = slice(2 * STARTS[step], 2 * (STARTS[step] + SIZES[step]))
        turned = pltpu.roll(beams[slot, lines].reshape(span, LANES).astype(jnp.float32), 96, 1)
        above = pltpu.roll(turned, span - 1, 0)
        last = lax.rem(iota((span, LANES), 0), GROUPS) == GROUPS - 1
        new = jnp.where(iota((span, LANES), 1) < 96, turned, jnp.where(last, 0.0, above))
        beams[slot, lines] = new.astype(jnp.bfloat16).reshape(2 * SIZES[step], GROUPS, LANES)

    def correlate(step):
        for way in range(2):
            send_edge(step, way).wait()

        @pl.when(d == 1)
        def _():
            passed_end(1, step)

        @pl.when((d == 1) | (d == TMS - 2))
        def _():
            passed_end(2, step)

        size = SIZES[step]
        span = size * ROWS
        lane = iota((span, LANES), 1)
        offset = iota((span, LANES), 0)
        lines = slice(2 * STARTS[step], 2 * (STARTS[step] + size))
        three = [beams[slot, lines].reshape(span, LANES) for slot in range(3)]
        for c in range(4):
            here, n1, n2 = [
                pltpu.roll(v, shift, 1) if shift else v
                for v, shift in ((v, (128 + 32 * (j - c)) % 128) for j, v in enumerate(three))
            ]
            mixed = jnp.where(lane < 32, here, jnp.where(lane < 64, n1, n2))
            mixed = mixed.reshape(size, ROWS, LANES) * signs[c * ROWS : (c + 1) * ROWS, :][None]
            coded[0:size, :, c] = mixed.reshape(size, 2, GROUPS, LANES)
        grams = []
        low = iota((256, LANES), 1) < 32
        for k in range(size):
            later = coded[k].reshape(256, LANES)
            turned = jnp.concatenate([-later[128:], later[:128]], 0)
            base = jnp.where(low, later, pltpu.roll(turned, 32, 1))
            gram = lax.dot_general(
                base, later, (((0,), (0,)), ((), ())), preferred_element_type=jnp.float32
            )
            real = jnp.concatenate(
                [pltpu.roll(gram[r : r + 8], 127 - r, 1) for r in (0, 8, 16, 24)], 0
            )
            imag = jnp.concatenate(
                [pltpu.roll(gram[r + 32 : r + 40], (191 - r) % 128, 1) for r in (0, 8, 16, 24)], 0
            )
            grams += [real, imag]
        gram = jnp.concatenate(grams, 0)
        for bit in (1, 2, 4):
            gram = jnp.where((offset & bit) > 0, pltpu.roll(gram, LANES - bit, 1), gram)
        gram = gram.reshape(size, 2, 32, LANES)
        skewed[0 : size * 32] = jnp.where(
            iota((size, 32, LANES), 2) < LAGS, gram[:, 0], gram[:, 1]
        ).reshape(size * 32, LANES)
        even = skewed[pl.ds(0, size * 16, stride=2), :]
        pairs = even + skewed[pl.ds(1, size * 16, stride=2), :]
        for k in range(size):
            place = (STARTS[step] + k) * LANES
            row_sec[z, :, place : place + LANES] = pairs[16 * k : 16 * k + 16].astype(
                jnp.bfloat16
            )

    def cols_of(step):
        return pl.ds(STARTS[step] * LANES, SIZES[step] * LANES)

    def send_z(step, i):
        return pltpu.make_async_remote_copy(
            src_ref=row_sec.at[z, :, cols_of(step)],
            dst_ref=row_sec.at[z, :, cols_of(step)],
            send_sem=z_send.at[step, i - 1],
            recv_sem=z_recv.at[step, i - 1],
            device_id=z_to(i),
            device_id_type=MESH,
        )

    def send_gates(step, i):
        return pltpu.make_async_remote_copy(
            src_ref=picked.at[lax.rem(d + i, 8), :, cols_of(step)],
            dst_ref=gate_part.at[i - 1, :, cols_of(step)],
            send_sem=g_send.at[step, i - 1],
            recv_sem=g_recv.at[step, i - 1],
            device_id=row_to(i),
            device_id_type=MESH,
        )

    fetch_gates.wait()
    gate_row = z * 32 + iota((32, NSEC), 0)
    named = (raw_gates[...] == gate_row).astype(jnp.bfloat16)
    col = iota((NSEC, 64), 1)
    origin = lax.rem(col // 16 * 8 + lax.rem(d, 8) + TMS - 2 * core, 16)
    section = 16 * origin + lax.rem(col, 16)
    chosen = (iota((NSEC, 64), 0) == section).astype(jnp.bfloat16)
    scale = 1.0 / math.sqrt(TMS * T_DEV / GATES)
    gate_hot = jnp.dot(named, chosen, preferred_element_type=jnp.float32).astype(jnp.bfloat16)

    def route(step):
        for i in (1, 2, 3):
            send_z(step, i).wait_recv()
        gathered = row_sec[:, :, cols_of(step)].reshape(64, SIZES[step] * LANES)
        gates = jnp.dot(gate_hot, gathered, preferred_element_type=jnp.float32) * scale
        for k in range(8):
            picked[k, :, cols_of(step)] = gates[4 * k : 4 * k + 4]
        for i in range(1, 8):
            send_gates(step, i).start()

    def finish(step):
        total = picked[lax.rem(d, 8), :, cols_of(step)]
        for i in range(1, 8):
            send_gates(step, i).wait_recv()
            total += gate_part[i - 1, :, cols_of(step)]
        out[:, cols_of(step)] = total

    level = level_of(lax.fori_loop(0, blocks, form, nothing))
    pl.semaphore_wait(barrier, len(met))
    for step in range(STEPS):
        launch(step)
    for step in range(STEPS):
        relay(step)
    for step in range(STEPS + 2):
        if step < STEPS:
            settle(step)
            share(step)
        if step >= 2:
            correlate(step - 2)
            for i in (1, 2, 3):
                send_z(step - 2, i).start()
    for step in range(STEPS):
        route(step)
    for step in range(STEPS):
        finish(step)

    for step in range(STEPS):
        for way in range(2):
            send_far(step, way).wait_send()
            send_near(step, way).wait_send()
        for i in (1, 2, 3):
            send_z(step, i).wait_send()
        for i in range(1, 8):
            send_gates(step, i).wait_send()


def body(streams, beam_weights, code_signs, gate_map):
    dma = pltpu.SemaphoreType.DMA
    channels = streams.shape[1]
    tiles = streams.reshape(2, channels, GROUPS, LANES).transpose(1, 2, 0, 3)
    paired = beam_weights.transpose(1, 0, 2)
    f32, bf16, i16 = jnp.float32, jnp.bfloat16, jnp.int16
    vmem = pl.BlockSpec(memory_space=pltpu.VMEM)
    hbm = pl.BlockSpec(memory_space=pltpu.HBM)
    summed = pl.pallas_call(
        kernel,
        out_shape=jax.ShapeDtypeStruct((4, WIDE), f32),
        in_specs=[hbm, hbm, vmem, hbm],
        out_specs=vmem,
        scratch_shapes=[
            pltpu.VMEM((GROUPS, channels, 2, LANES), bf16),
            pltpu.VMEM((100, 2, channels), bf16),
            pltpu.VMEM((1, NSEC), jnp.int32),
            pltpu.VMEM((2, 200, WEIGHT_TILES * LANES), bf16),
            pltpu.VMEM((200, WEIGHT_TILES * BLOCK), bf16),
            pltpu.VMEM((100 * ROWS, LANES), f32),
            pltpu.VMEM((2, BEAMS * GROUPS + 16 * STEPS, LANES), i16),
            pltpu.VMEM((2, BEAMS * ROWS + 16 * STEPS, LANES), i16),
            pltpu.VMEM((3, 2 * BEAMS, GROUPS, LANES), bf16),
            pltpu.VMEM((256, LANES), bf16),
            pltpu.VMEM((MOST, 2, 4, GROUPS, LANES), bf16),
            pltpu.VMEM((MOST * 32, LANES), f32),
            pltpu.VMEM((4, 16, WIDE), bf16),
            pltpu.VMEM((8, 4, WIDE), f32),
            pltpu.VMEM((7, 4, WIDE), f32),
            pltpu.VMEM((2, BEAMS * GROUPS + 16 * STEPS, LANES), i16),
            pltpu.VMEM((2, BEAMS * ROWS + 16 * STEPS, LANES), i16),
            dma((GROUPS,)), dma((2,)),
            dma((STEPS, 2)), dma((STEPS, 2)), dma((STEPS, 2)), dma((STEPS, 2)),
            dma((STEPS, 2)), dma((STEPS, 2)),
            dma((STEPS, 3)), dma((STEPS, 3)), dma((STEPS, 7)), dma((STEPS, 7)),
        ],
        compiler_params=pltpu.CompilerParams(
            collective_id=0, has_side_effects=True, vmem_limit_bytes=48 * 2**20
        ),
    )(tiles, paired, code_signs.T, gate_map.reshape(1, NSEC))
    return summed.reshape(4, BEAMS, LANES)


def solution(mesh):
    placed = (P(None, "sub", "tm"), P(None, None, "sub"), P(), P())
    return jax.shard_map(
        body, mesh=mesh, in_specs=placed, out_specs=P("tm", "sub", None), check_vma=False
    )
```

```python
import functools
import math

import jax
import jax.numpy as jnp
from jax import lax
from jax.experimental import pallas as pl
from jax.experimental.pallas import tpu as pltpu
from jax.sharding import PartitionSpec as P

PKT = 32
IPP_LEN = 512
LAGS = 64
NCODES = 32
NBAUD = 16
BAUD_LEN = 8
SEC_LEN = 2
GATES = 128
NSEC = 256
LANES = 128
SUBS = 4
TMS = 32
BEAMS = 25
T_DEV = 4096
GROUPS = T_DEV // LANES
ROWS = 2 * GROUPS
SPAN = 4
WEIGHT_TILES = 5
SIZES = (4, 4, 4, 4, 3, 3, 3)
STARTS = (0, 4, 8, 12, 16, 19, 22)
STEPS = len(SIZES)
MOST = max(SIZES)
BLOCK = 256
WIDE = BEAMS * LANES
BITS = 14.9
MESH = pl.DeviceIdType.MESH


def iota(shape, dim):
    return lax.broadcasted_iota(jnp.int32, shape, dim)


def kernel(
    streams, weights, code_signs, gate_map, out,
    held, raw_weights, raw_gates, plain, block_rows, sums, early, late, beams, signs,
    coded, skewed, row_sec, picked, gate_part, far_out, near_out,
    in_sem, w_sem, a_send, a_recv, b_send, b_recv, h_send, h_recv, z_send, z_recv, g_send, g_recv,
):
    y = lax.axis_index("sub")
    d = lax.axis_index("tm")
    z = d // 8
    core = lax.rem(d, 2)
    based = lax.rem(d + TMS - 2 * core, TMS)

    def ring(step):
        return (y, lax.rem(d + step + TMS, TMS))

    def sub_to(step):
        return (lax.rem(y + step, SUBS), d)

    def z_to(step):
        return (y, lax.rem(z + step, 4) * 8 + lax.rem(d, 8))

    def row_to(step):
        return (y, z * 8 + lax.rem(d + step, 8))

    def fetch(i):
        return pltpu.make_async_copy(streams.at[:, i], held.at[i], in_sem.at[i])

    fetch_weights = pltpu.make_async_copy(weights, raw_weights, w_sem.at[0])
    fetch_gates = pltpu.make_async_copy(gate_map, raw_gates, w_sem.at[1])
    fetch_weights.start()
    for i in range(GROUPS):
        fetch(i).start()
    fetch_gates.start()

    barrier = pltpu.get_barrier_semaphore()
    met = [sub_to(1), sub_to(3), ring(-2), ring(2)]
    met += [z_to(i) for i in (1, 2, 3)] + [row_to(i) for i in range(1, 8)]
    for device in met:
        pl.semaphore_signal(barrier, inc=1, device_id=device, device_id_type=MESH)

    channels = weights.shape[2]
    fetch_weights.wait()
    stacked = raw_weights[...].reshape(2 * weights.shape[0], channels)
    wide_rows = stacked.astype(jnp.float32)
    count = wide_rows.shape[0]
    odd = lax.rem(iota(wide_rows.shape, 0), 2) == 1
    turned_rows = jnp.where(odd, pltpu.roll(wide_rows, 1, 0), -pltpu.roll(wide_rows, count - 1, 0))
    plain[...] = jnp.zeros_like(plain)
    plain[0, :, 0:channels] = stacked
    plain[1, :, 0:channels] = turned_rows.astype(jnp.bfloat16)
    source = iota((BLOCK, BLOCK), 0)
    spread = (
        2 * lax.rem(source, LANES) + source // LANES == iota((BLOCK, BLOCK), 1)
    ).astype(jnp.bfloat16)
    for t in range(WEIGHT_TILES):
        cols = slice(t * LANES, (t + 1) * LANES)
        pair = jnp.concatenate([plain[0, :, cols], plain[1, :, cols]], 1)
        block_rows[:, t * BLOCK : (t + 1) * BLOCK] = jnp.dot(
            pair, spread, preferred_element_type=jnp.float32
        ).astype(jnp.bfloat16)
    samples = held.reshape(GROUPS, 2 * channels, LANES)

    def form(i, carry):
        for h in range(SPAN):
            fetch(SPAN * i + h).wait()
        product = jnp.dot(
            block_rows[:, 0 : 2 * channels],
            jnp.concatenate([samples[SPAN * i + h] for h in range(SPAN)], 1),
            preferred_element_type=jnp.float32,
        )
        for h in range(SPAN):
            place = SPAN * i + h
            sums[pl.ds(place, count, stride=GROUPS), :] = product[:, h * LANES : (h + 1) * LANES]
        top = jnp.max(jnp.abs(product).reshape(count // 8, 8, SPAN * LANES), axis=0)
        return jnp.maximum(carry, top)

    nothing = jnp.zeros((8, SPAN * LANES), jnp.float32)
    blocks = GROUPS // SPAN

    def level_of(top):
        most = jnp.maximum(jnp.max(top, axis=(0, 1), keepdims=True), 1e-30)
        return jnp.broadcast_to(jnp.ceil(jnp.log2(most)), (16, LANES))

    def rows_of(owner, step):
        return pl.multiple_of((owner * BEAMS + STARTS[step]) * ROWS, ROWS)

    def packed(value, power):
        steps = value.reshape(-1, 16, LANES) * jnp.exp2(BITS - power)[None]
        return jnp.round(steps).astype(jnp.int32).astype(jnp.int16).reshape(-1, LANES)

    def unpacked(ref, count):
        power = ref[count : count + 16, :].astype(jnp.int32).astype(jnp.float32)
        steps = ref[0:count, :].astype(jnp.int32).astype(jnp.float32)
        value = steps.reshape(-1, 16, LANES) * jnp.exp2(power - BITS)[None]
        return value.reshape(count, LANES), power

    def ways(way):
        return 1 if way == 0 else 3

    def send_far(step, way):
        half = SIZES[step] * GROUPS
        rows = pl.ds(STARTS[step] * GROUPS + 16 * step, half + 16)
        return pltpu.make_async_remote_copy(
            src_ref=far_out.at[way, rows],
            dst_ref=early.at[way, rows],
            send_sem=a_send.at[step, way],
            recv_sem=a_recv.at[step, way],
            device_id=sub_to(ways(way)),
            device_id_type=MESH,
        )

    def near_rows(step):
        return pl.ds(STARTS[step] * ROWS + 16 * step, SIZES[step] * ROWS + 16)

    def send_near(step, way):
        rows = near_rows(step)
        return pltpu.make_async_remote_copy(
            src_ref=near_out.at[way, rows],
            dst_ref=late.at[way, rows],
            send_sem=b_send.at[step, way],
            recv_sem=b_recv.at[step, way],
            device_id=sub_to(ways(way)),
            device_id_type=MESH,
        )

    def launch(step):
        half = SIZES[step] * GROUPS
        place = STARTS[step] * GROUPS + 16 * step
        for way in range(2):
            start = rows_of(lax.rem(y + 2, SUBS), step) + way * half
            far_out[way, place : place + half, :] = packed(sums[pl.ds(start, half), :], level)
            far_out[way, place + half : place + half + 16, :] = (
                level.astype(jnp.int32).astype(jnp.int16)
            )
            send_far(step, way).start()

    def send_edge(step, way):
        lines = pl.ds(2 * STARTS[step], 2 * SIZES[step])
        return pltpu.make_async_remote_copy(
            src_ref=beams.at[2 * core, lines],
            dst_ref=beams.at[1 if way == 0 else 2 - 2 * core, lines],
            send_sem=h_send.at[step, way],
            recv_sem=h_recv.at[step, way],
            device_id=(y, d + 1 - 2 * core) if way == 0 else ring(4 * core - 2),
            device_id_type=MESH,
        )

    row = iota((256, NCODES), 0)
    code_of = lax.rem(
        2 * lax.rem(4 * lax.rem(row, GROUPS) + row // 64, 16) + based // 16, NCODES
    )
    code_hot = (code_of == iota((256, NCODES), 1)).astype(jnp.bfloat16)
    lane16 = iota((NBAUD, LANES), 1)
    baud_hot = jnp.where(
        (lax.rem(4 * based + lane16 // BAUD_LEN, NBAUD) == iota((NBAUD, LANES), 0)) & (lane16 < 96),
        1.0,
        0.0,
    ).astype(jnp.bfloat16)
    table = (2 * code_signs[...] - 1).astype(jnp.float32).astype(jnp.bfloat16)
    by_code = lax.dot_general(
        code_hot, table, (((1,), (1,)), ((), ())), preferred_element_type=jnp.float32
    ).astype(jnp.bfloat16)
    signs[...] = jnp.dot(by_code, baud_hot, preferred_element_type=jnp.float32).astype(jnp.bfloat16)

    def relay(step):
        half = SIZES[step] * GROUPS
        place = STARTS[step] * GROUPS + 16 * step
        spot = STARTS[step] * ROWS + 16 * step
        for way in range(2):
            send_far(step, way).wait_recv()
            start = rows_of(lax.rem(y + ways(way), SUBS), step)
            passed, power = unpacked(early.at[way, pl.ds(place, half + 16)], half)
            both = jnp.maximum(power, level) + 1
            mine, rest = way * half, (1 - way) * half
            near_out[way, spot + mine : spot + mine + half, :] = packed(
                sums[pl.ds(start + mine, half), :] + passed, both
            )
            near_out[way, spot + rest : spot + rest + half, :] = packed(
                sums[pl.ds(start + rest, half), :], both
            )
            near_out[way, spot + 2 * half : spot + 2 * half + 16, :] = (
                both.astype(jnp.int32).astype(jnp.int16)
            )
            send_near(step, way).start()

    def settle(step):
        part = SIZES[step] * ROWS
        total = sums[pl.ds(rows_of(y, step), part), :]
        for way in range(2):
            send_near(step, way).wait_recv()
            total += unpacked(late.at[way, near_rows(step)], part)[0]
        beams[2 * core, 2 * STARTS[step] : 2 * (STARTS[step] + SIZES[step])] = total.astype(
            jnp.bfloat16
        ).reshape(2 * SIZES[step], GROUPS, LANES)

    def share(step):
        for way in range(2):
            send_edge(step, way).start()

    def passed_end(slot, step):
        span = SIZES[step] * ROWS
        lines = slice(2 * STARTS[step], 2 * (STARTS[step] + SIZES[step]))
        turned = pltpu.roll(beams[slot, lines].reshape(span, LANES).astype(jnp.float32), 96, 1)
        above = pltpu.roll(turned, span - 1, 0)
        last = lax.rem(iota((span, LANES), 0), GROUPS) == GROUPS - 1
        new = jnp.where(iota((span, LANES), 1) < 96, turned, jnp.where(last, 0.0, above))
        beams[slot, lines] = new.astype(jnp.bfloat16).reshape(2 * SIZES[step], GROUPS, LANES)

    def correlate(step):
        for way in range(2):
            send_edge(step, way).wait()

        @pl.when(d == 1)
        def _():
            passed_end(1, step)

        @pl.when((d == 1) | (d == TMS - 2))
        def _():
            passed_end(2, step)

        size = SIZES[step]
        span = size * ROWS
        lane = iota((span, LANES), 1)
        offset = iota((span, LANES), 0)
        lines = slice(2 * STARTS[step], 2 * (STARTS[step] + size))
        three = [beams[slot, lines].reshape(span, LANES) for slot in range(3)]
        for c in range(4):
            here, n1, n2 = [
                pltpu.roll(v, shift, 1) if shift else v
                for v, shift in ((v, (128 + 32 * (j - c)) % 128) for j, v in enumerate(three))
            ]
            mixed = jnp.where(lane < 32, here, jnp.where(lane < 64, n1, n2))
            mixed = mixed.reshape(size, ROWS, LANES) * signs[c * ROWS : (c + 1) * ROWS, :][None]
            coded[0:size, :, c] = mixed.reshape(size, 2, GROUPS, LANES)
        grams = []
        low = iota((256, LANES), 1) < 32
        for k in range(size):
            later = coded[k].reshape(256, LANES)
            turned = jnp.concatenate([-later[128:], later[:128]], 0)
            base = jnp.where(low, later, pltpu.roll(turned, 32, 1))
            gram = lax.dot_general(
                base, later, (((0,), (0,)), ((), ())), preferred_element_type=jnp.float32
            )
            real = jnp.concatenate(
                [pltpu.roll(gram[r : r + 8], 127 - r, 1) for r in (0, 8, 16, 24)], 0
            )
            imag = jnp.concatenate(
                [pltpu.roll(gram[r + 32 : r + 40], (191 - r) % 128, 1) for r in (0, 8, 16, 24)], 0
            )
            grams += [real, imag]
        gram = jnp.concatenate(grams, 0)
        for bit in (1, 2, 4):
            gram = jnp.where((offset & bit) > 0, pltpu.roll(gram, LANES - bit, 1), gram)
        gram = gram.reshape(size, 2, 32, LANES)
        skewed[0 : size * 32] = jnp.where(
            iota((size, 32, LANES), 2) < LAGS, gram[:, 0], gram[:, 1]
        ).reshape(size * 32, LANES)
        even = skewed[pl.ds(0, size * 16, stride=2), :]
        pairs = even + skewed[pl.ds(1, size * 16, stride=2), :]
        for k in range(size):
            place = (STARTS[step] + k) * LANES
            row_sec[z, :, place : place + LANES] = pairs[16 * k : 16 * k + 16].astype(
                jnp.bfloat16
            )

    def cols_of(step):
        return pl.ds(STARTS[step] * LANES, SIZES[step] * LANES)

    def send_z(step, i):
        return pltpu.make_async_remote_copy(
            src_ref=row_sec.at[z, :, cols_of(step)],
            dst_ref=row_sec.at[z, :, cols_of(step)],
            send_sem=z_send.at[step, i - 1],
            recv_sem=z_recv.at[step, i - 1],
            device_id=z_to(i),
            device_id_type=MESH,
        )

    def send_gates(step, i):
        return pltpu.make_async_remote_copy(
            src_ref=picked.at[lax.rem(d + i, 8), :, cols_of(step)],
            dst_ref=gate_part.at[i - 1, :, cols_of(step)],
            send_sem=g_send.at[step, i - 1],
            recv_sem=g_recv.at[step, i - 1],
            device_id=row_to(i),
            device_id_type=MESH,
        )

    fetch_gates.wait()
    gate_row = z * 32 + iota((32, NSEC), 0)
    named = (raw_gates[...] == gate_row).astype(jnp.bfloat16)
    col = iota((NSEC, 64), 1)
    origin = lax.rem(col // 16 * 8 + lax.rem(d, 8) + TMS - 2 * core, 16)
    section = 16 * origin + lax.rem(col, 16)
    chosen = (iota((NSEC, 64), 0) == section).astype(jnp.bfloat16)
    scale = 1.0 / math.sqrt(TMS * T_DEV / GATES)
    gate_hot = jnp.dot(named, chosen, preferred_element_type=jnp.float32).astype(jnp.bfloat16)

    def route(step):
        for i in (1, 2, 3):
            send_z(step, i).wait_recv()
        gathered = row_sec[:, :, cols_of(step)].reshape(64, SIZES[step] * LANES)
        gates = jnp.dot(gate_hot, gathered, preferred_element_type=jnp.float32) * scale
        for k in range(8):
            picked[k, :, cols_of(step)] = gates[4 * k : 4 * k + 4]
        for i in range(1, 8):
            send_gates(step, i).start()

    def finish(step):
        total = picked[lax.rem(d, 8), :, cols_of(step)]
        for i in range(1, 8):
            send_gates(step, i).wait_recv()
            total += gate_part[i - 1, :, cols_of(step)]
        out[:, cols_of(step)] = total

    level = level_of(lax.fori_loop(0, blocks, form, nothing))
    pl.semaphore_wait(barrier, len(met))
    for step in range(STEPS):
        launch(step)
    for step in range(STEPS):
        relay(step)
    for step in range(STEPS):
        settle(step)
        share(step)
    for step in range(STEPS):
        correlate(step)
        for i in (1, 2, 3):
            send_z(step, i).start()
    for step in range(STEPS):
        route(step)
    for step in range(STEPS):
        finish(step)

    for step in range(STEPS):
        for way in range(2):
            send_far(step, way).wait_send()
            send_near(step, way).wait_send()
        for i in (1, 2, 3):
            send_z(step, i).wait_send()
        for i in range(1, 8):
            send_gates(step, i).wait_send()


def body(streams, beam_weights, code_signs, gate_map):
    dma = pltpu.SemaphoreType.DMA
    channels = streams.shape[1]
    tiles = streams.reshape(2, channels, GROUPS, LANES).transpose(1, 2, 0, 3)
    paired = beam_weights.transpose(1, 0, 2)
    f32, bf16, i16 = jnp.float32, jnp.bfloat16, jnp.int16
    vmem = pl.BlockSpec(memory_space=pltpu.VMEM)
    hbm = pl.BlockSpec(memory_space=pltpu.HBM)
    summed = pl.pallas_call(
        kernel,
        out_shape=jax.ShapeDtypeStruct((4, WIDE), f32),
        in_specs=[hbm, hbm, vmem, hbm],
        out_specs=vmem,
        scratch_shapes=[
            pltpu.VMEM((GROUPS, channels, 2, LANES), bf16),
            pltpu.VMEM((100, 2, channels), bf16),
            pltpu.VMEM((1, NSEC), jnp.int32),
            pltpu.VMEM((2, 200, WEIGHT_TILES * LANES), bf16),
            pltpu.VMEM((200, WEIGHT_TILES * BLOCK), bf16),
            pltpu.VMEM((100 * ROWS, LANES), f32),
            pltpu.VMEM((2, BEAMS * GROUPS + 16 * STEPS, LANES), i16),
            pltpu.VMEM((2, BEAMS * ROWS + 16 * STEPS, LANES), i16),
            pltpu.VMEM((3, 2 * BEAMS, GROUPS, LANES), bf16),
            pltpu.VMEM((256, LANES), bf16),
            pltpu.VMEM((MOST, 2, 4, GROUPS, LANES), bf16),
            pltpu.VMEM((MOST * 32, LANES), f32),
            pltpu.VMEM((4, 16, WIDE), bf16),
            pltpu.VMEM((8, 4, WIDE), f32),
            pltpu.VMEM((7, 4, WIDE), f32),
            pltpu.VMEM((2, BEAMS * GROUPS + 16 * STEPS, LANES), i16),
            pltpu.VMEM((2, BEAMS * ROWS + 16 * STEPS, LANES), i16),
            dma((GROUPS,)), dma((2,)),
            dma((STEPS, 2)), dma((STEPS, 2)), dma((STEPS, 2)), dma((STEPS, 2)),
            dma((STEPS, 2)), dma((STEPS, 2)),
            dma((STEPS, 3)), dma((STEPS, 3)), dma((STEPS, 7)), dma((STEPS, 7)),
        ],
        compiler_params=pltpu.CompilerParams(
            collective_id=0, has_side_effects=True, vmem_limit_bytes=48 * 2**20
        ),
    )(tiles, paired, code_signs.T, gate_map.reshape(1, NSEC))
    return summed.reshape(4, BEAMS, LANES)


def solution(mesh):
    placed = (P(None, "sub", "tm"), P(None, None, "sub"), P(), P())
    return jax.shard_map(
        body, mesh=mesh, in_specs=placed, out_specs=P("tm", "sub", None), check_vma=False
    )
```
